32 devices in a mesh: section: 4 (over y, x), seq: 8 (over z, core).
Axes of the slice: x: 2, y: 2, z: 4, core: 2. Of those that a mesh axis runs over, the one named last changes fastest.
Arguments:
- inputs: bfloat16 [4, 4096, 1536], P(None, 'seq'), may hold values from -40 to 40
- weights: bfloat16 [2, 5, 1536, 1536], P(None, None, None, 'section'), may hold values from -0.0625 to 0.0625
- gains: float32 [2, 1536], replicated, may hold values from 0.1 to 1.9
Outputs:
- activations: bfloat16 [2, 4, 4096, 1536], P(None, None, 'seq', 'section')
The draws below stay inside these ranges and needn't reach their ends.
All inputs are finite; a program needn't handle non-finite values.
Results may differ from the reference program's by a relative error of at most 0.0044.
Values may be sent and summed in bfloat16 or wider, within the bound.
A program may use at most 128 MiB of HBM per device.

```python
import math
import jax
import jax.numpy as jnp
from jax import lax

C = 1536
KW = 5
LAYERS = 2
MICRO = 4
LEN = 4096


def draw_inputs(key, part):
    first, second, third = jax.random.split(jax.random.fold_in(key, 11), 3)
    chan = jnp.exp(jax.random.uniform(second, (1, 1, C), jnp.float32, math.log(0.3), math.log(3.0)))
    place = jnp.exp(jax.random.uniform(third, (MICRO, LEN, 1), jnp.float32, math.log(0.3), math.log(3.0)))
    base = jnp.clip(jax.random.normal(first, (MICRO, LEN, C), jnp.float32), -4.0, 4.0)
    return (base * chan * place).astype(jnp.bfloat16)


def levels(own_key, shape, shards, least, top_value):
    level = 1.0
    for axis_at, shards_of in shards:
        heights = jax.random.uniform(jax.random.fold_in(jax.random.fold_in(own_key, 6), axis_at), (shards_of,), jnp.float32, least / len(shards), top_value / len(shards))
        level = level * jnp.repeat(jnp.exp(heights), shape[axis_at] // shards_of).reshape((-1,) + (1,) * (len(shape) - 1 - axis_at))
    return level


def centred(own_key, shape, scale, reach, cuts=(), held_as=jnp.bfloat16):
    drawn = jax.random.normal(own_key, shape, jnp.float32) * scale
    if len(cuts) > 0:
        drawn = levels(own_key, shape, cuts, -0.22, 0.18) * drawn
    return jnp.clip(drawn, min=-reach, max=reach).astype(held_as)


def setup_inputs(seed: int = 0) -> dict:
    key_list = jax.random.split(jax.random.key(seed), 4)
    inputs = draw_inputs(jax.random.fold_in(key_list[3], 71), 0)
    weights = centred(key_list[1], (LAYERS, KW, C, C), (KW * C) ** -0.5, 0.0625, ((3, 4),))
    gains = jnp.clip(1.0 + 0.18 * jax.random.normal(key_list[2], (LAYERS, C), jnp.float32), 0.1, 1.9)
    return dict(inputs=inputs, weights=weights, gains=gains)


def block(current, kernel, gain):
    values = current.astype(jnp.float32)
    scale = lax.rsqrt(lax.optimization_barrier(jnp.mean(values * values, axis=-1, keepdims=True)) + 1e-06)
    hidden = jax.nn.gelu(values * scale * gain).astype(jnp.bfloat16)
    padded = jnp.pad(hidden, ((0, 0), (2, 2), (0, 0)))
    total = jnp.zeros((MICRO * LEN, C), jnp.float32)
    for k in range(KW):
        window = padded[:, k:k + LEN, :].reshape(MICRO * LEN, C)
        total = total + jnp.dot(window, kernel[k], preferred_element_type=jnp.float32)
    return (values + total.reshape(MICRO, LEN, C)).astype(jnp.bfloat16)

def reference(inputs, weights, gains):

    def layer(current, pair):
        kernel, gain = pair
        nxt = block(current, kernel, gain)
        return (nxt, nxt)
    final, stacked = lax.scan(layer, inputs, (weights, gains))
    return stacked
```

```python
import jax
import jax.numpy as jnp
from jax import lax
from jax.experimental import pallas as pl
from jax.experimental.pallas import tpu as pltpu
from jax.sharding import PartitionSpec as P

MESH = pl.DeviceIdType.MESH
HALO = 16
REACH = 2
EXTRA = 128


def with_halo(value, sides, width):
    for axis, dim in sides:
        count, length = (lax.axis_size(axis), value.shape[dim])
        up = [(i, (i + 1) % count) for i in range(count - 1)]
        down = [(j, i) for i, j in up]
        last = lax.slice_in_dim(value, length - width, length, axis=dim)
        initial = lax.slice_in_dim(value, 0, width, axis=dim)
        before = lax.ppermute(last, axis, up)
        after = lax.ppermute(initial, axis, down)
        value = jnp.concatenate([before, value, after], axis=dim)
    return value


def convolve(padded, kernel):
    count = padded.shape[1] - 4
    total = jnp.zeros((padded.shape[0], count, kernel.shape[2]), jnp.float32)
    for k in range(5):
        total = total + jnp.einsum(
            "brc,co->bro", padded[:, k : k + count], kernel[k], preferred_element_type=jnp.float32
        )
    return total


def normed(current, gain):
    values = current.astype(jnp.float32)
    scale = lax.rsqrt(jnp.mean(values * values, axis=-1, keepdims=True) + 1e-06)
    return jax.nn.gelu(values * scale * gain).astype(jnp.bfloat16)


def neighbours(hidden):
    return with_halo(hidden, (("seq", 1),), 2)


def plain(inputs, weights, gains):
    share = weights.shape[3]
    begin = lax.axis_index("section") * share
    hidden = normed(inputs, gains[0])
    conv = convolve(neighbours(hidden), weights[0])
    own = lax.dynamic_slice_in_dim(inputs, begin, share, 2)
    current = (own.astype(jnp.float32) + conv).astype(jnp.bfloat16)
    results = [current]
    kernel = weights[1]
    whole = lax.all_gather(current, "section", axis=2, tiled=True)
    conv = convolve(neighbours(normed(whole, gains[1])), kernel)
    current = (current.astype(jnp.float32) + conv).astype(jnp.bfloat16)
    results.append(current)
    return jnp.stack(results, axis=0)


def gelu(v):
    return 0.5 * v * (1.0 + jnp.tanh(v * (0.7978845608028654 + 0.035677408136300125 * (v * v))))


def chunk_ends(rows):
    tiles = rows // 16
    return [tiles * 11 // 32 * 16, tiles * 23 // 32 * 16, rows]


def schedule(count):
    early = {4 + 3 * m: m for m in range(count) if 4 + 3 * m < count}
    between = list(range(len(early), min(len(early) + 2, count)))
    rest = range(len(early) + len(between), count)
    late = {}
    for n, m in enumerate(rest):
        late.setdefault(max(0, min(2 * n + 1, m - 1)), []).append(m)
    return early, between, late


def fused_kernel(
    x, w, g, out, xe, hid, hid1, y, yx, wv, wx, gv, acts, last,
    gsem, wsem, xsem, hsend, hrecv, ssem, rsem, osem, lsem,
    tsend, trecv, zsend, zrecv, psend, precv,
):
    micro, rows, chans = x.shape
    taps, share = w.shape[1], w.shape[3]
    span = rows + 2 * HALO
    ends = chunk_ends(rows)
    begins = [0] + ends[:-1]
    parts = len(ends)
    count = parts * micro
    me, seq = lax.axis_index("section"), lax.axis_index("seq")
    nseq = lax.axis_size("seq")
    planes = nseq // 2
    plane, core = seq // 2, seq % 2
    partner = seq + 1 - 2 * core
    piece_rows = chans // nseq
    early, between, late = schedule(count)

    def ring(at):
        r = at // 2
        return 2 * r + (at % 2) * (1 - 2 * (r % 2)) + r % 2

    place = ring(me)
    right, left = ring((place + 1) % 4), ring((place + 3) % 4)
    over = ring((place + 2) % 4)

    gains = pltpu.make_async_copy(g, gv, gsem)

    def load(b):
        return pltpu.make_async_copy(x.at[b], xe.at[b, pl.ds(HALO, rows)], xsem.at[b])

    def weight(l, k):
        return pltpu.make_async_copy(w.at[l, k], wv.at[l, :, pl.ds(k * share, share)], wsem.at[l, k])

    gains.start()
    load(0).start()
    for k in range(taps):
        weight(0, k).start()

    barrier = pltpu.get_barrier_semaphore()
    for to in (right, left):
        pl.semaphore_signal(barrier, inc=1, device_id=(to, seq), device_id_type=MESH)

    def greet(reach):
        @pl.when(seq >= reach)
        def _():
            pl.semaphore_signal(barrier, inc=1, device_id=(me, seq - reach), device_id_type=MESH)

        @pl.when(seq < nseq - reach)
        def _():
            pl.semaphore_signal(barrier, inc=1, device_id=(me, seq + reach), device_id_type=MESH)

    greet(1)
    greet(2)
    peers = 2
    for reach in (1, 2):
        peers = peers + jnp.where(seq >= reach, 1, 0) + jnp.where(seq < nseq - reach, 1, 0)
    pl.semaphore_wait(barrier, peers)

    def halo_up(b):
        return pltpu.make_async_remote_copy(
            src_ref=x.at[b, pl.ds(rows - HALO, HALO), :],
            dst_ref=xe.at[b, pl.ds(0, HALO), :],
            send_sem=hsend.at[0, b],
            recv_sem=hrecv.at[0, b],
            device_id=(me, seq + 1),
            device_id_type=MESH,
        )

    def halo_down(b):
        return pltpu.make_async_remote_copy(
            src_ref=x.at[b, pl.ds(0, HALO), :],
            dst_ref=xe.at[b, pl.ds(HALO + rows, HALO), :],
            send_sem=hsend.at[1, b],
            recv_sem=hrecv.at[1, b],
            device_id=(me, seq - 1),
            device_id_type=MESH,
        )

    def tap(k):
        return pltpu.make_async_remote_copy(
            src_ref=w.at[0, k, pl.ds(seq * piece_rows, piece_rows), pl.ds(0, EXTRA)],
            dst_ref=wx.at[pl.ds(seq * piece_rows, piece_rows), pl.ds(k * EXTRA, EXTRA)],
            send_sem=tsend.at[k],
            recv_sem=trecv.at[k],
            device_id=(right, seq),
            device_id_type=MESH,
        )

    groups = ((0, 3), (3, taps))

    def block(index, n):
        low, high = groups[n]
        return wx.at[
            pl.ds(pl.multiple_of(index * piece_rows, 8), piece_rows),
            pl.ds(low * EXTRA, (high - low) * EXTRA),
        ]

    def spread(at, n, way, to):
        source = 2 * at + core
        return pltpu.make_async_remote_copy(
            src_ref=block(source, n),
            dst_ref=block(source, n),
            send_sem=zsend.at[way, at, n],
            recv_sem=zrecv.at[at, n],
            device_id=(me, to),
            device_id_type=MESH,
        )

    def swap(at, n):
        source = 2 * at + core
        return pltpu.make_async_remote_copy(
            src_ref=block(source, n),
            dst_ref=block(source, n),
            send_sem=psend.at[at, n],
            recv_sem=precv.at[at, n],
            device_id=(me, partner),
            device_id_type=MESH,
        )

    def swapped(at, n):
        source = 2 * at + 1 - core
        return pltpu.make_async_remote_copy(
            src_ref=block(source, n),
            dst_ref=block(source, n),
            send_sem=psend.at[at, n],
            recv_sem=precv.at[at, n],
            device_id=(me, partner),
            device_id_type=MESH,
        )

    def spread_own(n):
        for k in range(*groups[n]):
            tap(k).wait_recv()

        @pl.when(plane < planes - 1)
        def _():
            spread(plane, n, 0, seq + 2).start()

        @pl.when(plane > 0)
        def _():
            spread(plane, n, 1, seq - 2).start()

        swap(plane, n).start()

    def spread_far(d, n):
        @pl.when(plane >= d)
        def _():
            spread(plane - d, n, 0, seq).wait_recv()

            @pl.when(plane < planes - 1)
            def _():
                spread(plane - d, n, 0, seq + 2).start()

            swap(plane - d, n).start()

        @pl.when(plane < planes - d)
        def _():
            spread(plane + d, n, 1, seq).wait_recv()

            @pl.when(plane > 0)
            def _():
                spread(plane + d, n, 1, seq - 2).start()

            swap(plane + d, n).start()

    def spread_sent():
        for n in range(len(groups)):
            for k in range(*groups[n]):
                tap(k).wait_send()
            for at in range(planes):
                swap(at, n).wait_send()

                @pl.when((plane >= at) & (plane < planes - 1))
                def _():
                    spread(at, n, 0, seq + 2).wait_send()

                @pl.when((plane <= at) & (plane > 0))
                def _():
                    spread(at, n, 1, seq - 2).wait_send()

    @pl.when(seq < nseq - 1)
    def _():
        for b in range(micro):
            halo_up(b).start()

    @pl.when(seq > 0)
    def _():
        for b in range(micro):
            halo_down(b).start()

    for k in range(taps):
        tap(k).start()

    @pl.when(seq == 0)
    def _():
        xe[:, 0:HALO, :] = jnp.zeros((micro, HALO, chans), jnp.bfloat16)

    @pl.when(seq == nseq - 1)
    def _():
        xe[:, HALO + rows : span, :] = jnp.zeros((micro, HALO, chans), jnp.bfloat16)

    def send(origin, c, way, to):
        b, t = c // parts, c % parts
        size = ends[t] - begins[t] + (8 if t == parts - 1 else 0)
        low, high = ((EXTRA, share), (0, share), (EXTRA, share), (0, EXTRA))[way]
        ref = acts.at[origin, b, pl.ds(begins[t], size), pl.ds(low, high - low)]
        return pltpu.make_async_remote_copy(
            src_ref=ref,
            dst_ref=ref,
            send_sem=ssem.at[way, c],
            recv_sem=rsem.at[way, c],
            device_id=(to, seq),
            device_id_type=MESH,
        )

    def direct(c):
        send(me, c, 0, right).start()
        send(me, c, 1, left).start()

    def forward(c):
        send(left, c, 0, left).wait_recv()
        send(left, c, 2, right).start()
        send(right, c, 1, right).wait_recv()
        send(right, c, 3, left).start()
        if c + 3 < count:
            direct(c + 3)

    def arrived(b, t):
        size = ends[t] - begins[t] + (8 if t == parts - 1 else 0)
        c = b * parts + t
        for way, low, high in ((2, EXTRA, share), (3, 0, EXTRA)):
            ref = acts.at[over, b, pl.ds(begins[t], size), pl.ds(low, high - low)]
            pltpu.make_async_remote_copy(
                src_ref=ref,
                dst_ref=ref,
                send_sem=ssem.at[way, c],
                recv_sem=rsem.at[way, c],
                device_id=(right, seq),
                device_id_type=MESH,
            ).wait_recv()

    tile = 16

    def activate(v, l):
        scale = lax.rsqrt(jnp.mean(v * v, axis=-1, keepdims=True) + 1e-06)
        return gelu(v * scale * gv[l : l + 1, :]).astype(jnp.bfloat16)

    def merged(b, columns):
        top = xe[b, 0:HALO, columns].astype(jnp.float32)[8:16, :]
        bottom = xe[b, HALO + rows : span, columns].astype(jnp.float32)[0:8, :]
        row = lax.broadcasted_iota(jnp.int32, top.shape, 0)
        return jnp.where(row < 4, bottom, top)

    def product(dst, src, kernel, at, begin, end, wide, ready=None):
        step = 512
        for n in range(0, wide, step):
            size = min(step, wide - n)
            if ready is not None:
                ready(n, n + size)
            dst[begin + at : end + at, n : n + size] = jnp.dot(
                src(begin, end), kernel(n, size), preferred_element_type=jnp.float32
            )

    def gather_taps(src, at, width, stride):
        total = None
        block = src[pl.ds(pl.multiple_of(at + 16, 8), tile + 16), :]
        for k in range(taps):
            term = block[8 - REACH + k : 8 - REACH + k + tile, k * stride : k * stride + width]
            total = term if total is None else total + term
        return total

    def each(begin, end, body):
        @pl.loop(0, (end - begin) // tile, unroll=True)
        def _(i):
            body(pl.multiple_of(begin + i * tile, tile))

    mine = pl.ds(pl.multiple_of(me * share, 128), share)
    theirs = pl.ds(pl.multiple_of(left * share, 128), EXTRA)

    def conv_first(b, t, src, owner, columns, width, stride):
        def body(at):
            value = xe[b, pl.ds(at + HALO, tile), columns].astype(jnp.float32)
            value = value + gather_taps(src, at, width, stride)
            acts[owner, b, pl.ds(at, tile), 0:width] = value.astype(jnp.bfloat16)

        each(begins[t], ends[t], body)
        if t == parts - 1:
            top = gather_taps(src, -8, width, stride)[0:8, :]
            bottom = gather_taps(src, rows - 8, width, stride)[8:16, :]
            row = lax.broadcasted_iota(jnp.int32, top.shape, 0)
            value = merged(b, columns) + jnp.where(row < 4, bottom, top)
            inside = ((row < 4) & (seq < nseq - 1)) | ((row >= 4) & (seq > 0))
            value = jnp.where(inside, value, 0.0)
            value = jnp.concatenate([value, jnp.zeros_like(value)], axis=0)
            acts[owner, b, rows : rows + 16, 0:width] = value.astype(jnp.bfloat16)

    def bounds(t):
        begin = 0 if t == 0 else ends[t - 1] + 2 * HALO
        end = HALO + rows if t == parts - 1 else ends[t] + 2 * HALO
        return begin, end

    def first(b, t):
        begin, end = bounds(t)
        if t == 0:
            load(b).wait()

            @pl.when(b == 0)
            def _():
                gains.wait()

        def own(at):
            hid[b, pl.ds(at, tile), :] = activate(xe[b, pl.ds(at, tile), :].astype(jnp.float32), 0)

        each(max(begin, HALO), end, own)
        if t == 0:

            @pl.when(seq > 0)
            def _():
                halo_up(b).wait_recv()

            @pl.when(seq < nseq - 1)
            def _():
                halo_down(b).wait_recv()

            edge = merged(b, slice(None))
            hid[b, 0:HALO, :] = activate(jnp.concatenate([jnp.zeros_like(edge), edge], axis=0), 0)

        def ready(low, high):
            @pl.when(b == 0)
            def _():
                for k in range(taps):
                    if low <= k * share < high:
                        weight(0, k).wait()

        product(
            y, lambda p, q: hid[b, p:q, :], lambda n, s: wv[0, :, n : n + s], 8, begin, end,
            taps * share, ready if t == 0 else None,
        )
        if t == 0:
            y[HALO + 8 + rows : HALO + 16 + rows, :] = y[HALO : HALO + 8, :]

            @pl.when(b == 0)
            def _():
                for other in range(1, micro):
                    load(other).start()
                for k in range(taps):
                    weight(1, k).start()

        conv_first(b, t, y, me, mine, share, share)

    def extra(b, t):
        begin, end = bounds(t)
        product(
            yx, lambda p, q: hid[b, p:q, :], lambda n, s: wx[:, n : n + s], 8, begin, end,
            taps * EXTRA,
        )
        if t == 0:
            yx[HALO + 8 + rows : HALO + 16 + rows, :] = yx[HALO : HALO + 8, :]
        conv_first(b, t, yx, left, theirs, EXTRA, EXTRA)

    def second(b, t):
        end = ends[t] + (HALO if t == parts - 1 else 0)

        def own(at):
            pieces = [acts[s, b, pl.ds(at, tile), :].astype(jnp.float32) for s in range(4)]
            hid1[pl.ds(at, tile), :] = activate(jnp.concatenate(pieces, axis=-1), 1)

        each(begins[t], ends[t], own)
        if t == parts - 1:
            pieces = [acts[s, b, rows : rows + HALO, :].astype(jnp.float32) for s in range(4)]
            edge = jnp.concatenate(pieces, axis=-1)[0:8, :]
            hid1[rows : rows + HALO, :] = activate(
                jnp.concatenate([edge, jnp.zeros_like(edge)], axis=0), 1
            )
        product(
            y, lambda p, q: hid1[p:q, :], lambda n, s: wv[1, :, n : n + s], 24, begins[t], end,
            taps * share,
        )
        if t == parts - 1:
            y[HALO : HALO + 8, :] = y[HALO + 8 + rows : HALO + 16 + rows, :]

        def body(at):
            value = acts[me, b, pl.ds(at, tile), :].astype(jnp.float32)
            value = value + gather_taps(y, at, share, share)
            last[b, pl.ds(at, tile), :] = value.astype(jnp.bfloat16)

        each(max(begins[t] - tile, tile), rows if t == parts - 1 else ends[t] - tile, body)
        if t == parts - 1:
            body(0)

    def out_first(b):
        return pltpu.make_async_copy(acts.at[me, b, pl.ds(0, rows), :], out.at[0, b], osem.at[b])

    cuts = (0, tile, ends[-2] - tile, rows)

    def out_last(b, n):
        part = pl.ds(cuts[n], cuts[n + 1] - cuts[n])
        return pltpu.make_async_copy(last.at[b, part], out.at[1, b, part], lsem.at[b, n])

    def at_step(b, t, table, act):
        for bb in range(micro):
            for m in table.get(bb * parts + t, ()):
                pl.when(b == bb)(lambda m=m: act(m))

    errands = {}
    for n in range(len(groups)):
        errands.setdefault(1 + 2 * n, []).append(("own", 0, n))
        for d in range(1, planes):
            errands.setdefault(min(5 + 4 * (d - 1) + n, count), []).append(("far", d, n))

    def errand(e):
        kind, d, n = e
        if kind == "own":
            spread_own(n)
        else:
            spread_far(d, n)

    @pl.loop(0, micro)
    def _(b):
        for t in range(parts):
            first(b, t)
            at_step(b, t, {c: (c,) for c in range(3)}, direct)
            at_step(b, t, {p: (m,) for p, m in early.items()}, forward)
            at_step(b, t, errands, errand)
        out_first(b).start()

    for m in between[:1]:
        forward(m)
    for e in errands.get(count, ()):
        errand(e)
    for m in between[1:]:
        forward(m)
    for n in range(len(groups)):
        for at in range(planes):
            swapped(at, n).wait_recv()
    for k in range(taps):
        weight(1, k).wait()

    @pl.loop(0, micro)
    def _(b):
        for t in range(parts):
            at_step(b, t, late, forward)
            extra(b, t)
            arrived(b, t)
            second(b, t)
            if t == parts - 2:
                out_last(b, 1).start()
        out_last(b, 0).start()
        out_last(b, 2).start()

    @pl.when(seq < nseq - 1)
    def _():
        for b in range(micro):
            halo_up(b).wait_send()

    @pl.when(seq > 0)
    def _():
        for b in range(micro):
            halo_down(b).wait_send()

    spread_sent()
    for c in range(count):
        send(me, c, 0, right).wait_send()
        send(me, c, 1, left).wait_send()
        send(left, c, 2, right).wait_send()
        send(right, c, 3, left).wait_send()

    @pl.loop(0, micro)
    def _(b):
        out_first(b).wait()
        for n in range(3):
            out_last(b, n).wait()


def fused(inputs, weights, gains):
    micro, rows, chans = inputs.shape
    layers, taps, _, share = weights.shape
    span = rows + 2 * HALO
    count = len(chunk_ends(rows)) * micro
    planes = lax.axis_size("seq") // 2
    dma = pltpu.SemaphoreType.DMA
    hbm = pl.BlockSpec(memory_space=pltpu.HBM)
    return pl.pallas_call(
        fused_kernel,
        out_shape=jax.ShapeDtypeStruct((layers, micro, rows, share), jnp.bfloat16),
        in_specs=[hbm, hbm, hbm],
        out_specs=pl.BlockSpec(memory_space=pl.ANY),
        scratch_shapes=[
            pltpu.VMEM((micro, span, chans), jnp.bfloat16),
            pltpu.VMEM((micro, rows + HALO, chans), jnp.bfloat16),
            pltpu.VMEM((rows + HALO, chans), jnp.bfloat16),
            pltpu.VMEM((rows + 40, taps * share), jnp.float32),
            pltpu.VMEM((rows + 40, taps * EXTRA), jnp.float32),
            pltpu.VMEM((2, chans, taps * share), jnp.bfloat16),
            pltpu.VMEM((chans, taps * EXTRA), jnp.bfloat16),
            pltpu.VMEM(gains.shape, jnp.float32),
            pltpu.VMEM((4, micro, rows + HALO, share), jnp.bfloat16),
            pltpu.VMEM((micro, rows, share), jnp.bfloat16),
            dma,
            dma((2, taps)),
            dma((micro,)),
            dma((2, micro)),
            dma((2, micro)),
            dma((4, count)),
            dma((4, count)),
            dma((micro,)),
            dma((micro, 3)),
            dma((taps,)),
            dma((taps,)),
            dma((2, planes, 2)),
            dma((planes, 2)),
            dma((planes, 2)),
            dma((planes, 2)),
        ],
        compiler_params=pltpu.CompilerParams(
            collective_id=0, has_side_effects=True, vmem_limit_bytes=50 * 1024 * 1024
        ),
    )(inputs, weights, gains)


def local(inputs, weights, gains):
    micro, rows, chans = inputs.shape
    layers, taps, _, share = weights.shape
    nseq = lax.axis_size("seq")
    square = lax.axis_size("section") == 4 and layers == 2 and nseq % 2 == 0 and nseq > 2
    wide = share % 128 == 0 and share > EXTRA and chans % (16 * nseq) == 0
    if square and wide and taps == 5 and micro > 1 and rows % 512 == 0:
        return fused(inputs, weights, gains)
    return plain(inputs, weights, gains)


def solution(mesh):
    in_specs = (P(None, "seq", None), P(None, None, None, "section"), P())
    out_specs = P(None, None, "seq", "section")
    return jax.shard_map(local, mesh=mesh, in_specs=in_specs, out_specs=out_specs, check_vma=False)
```

```python
import functools
import jax
import jax.numpy as jnp
from jax import lax
from jax.experimental import pallas as pl
from jax.experimental.pallas import tpu as pltpu
from jax.sharding import PartitionSpec as P

MESH = pl.DeviceIdType.MESH
HALO = 16
REACH = 2
EXTRA = 128


def with_halo(value, sides, width):
    for axis, dim in sides:
        count, length = (lax.axis_size(axis), value.shape[dim])
        up = [(i, (i + 1) % count) for i in range(count - 1)]
        down = [(j, i) for i, j in up]
        last = lax.slice_in_dim(value, length - width, length, axis=dim)
        initial = lax.slice_in_dim(value, 0, width, axis=dim)
        before = lax.ppermute(last, axis, up)
        after = lax.ppermute(initial, axis, down)
        value = jnp.concatenate([before, value, after], axis=dim)
    return value


def convolve(padded, kernel):
    count = padded.shape[1] - 4
    total = jnp.zeros((padded.shape[0], count, kernel.shape[2]), jnp.float32)
    for k in range(5):
        total = total + jnp.einsum(
            "brc,co->bro", padded[:, k : k + count], kernel[k], preferred_element_type=jnp.float32
        )
    return total


def normed(current, gain):
    values = current.astype(jnp.float32)
    scale = lax.rsqrt(jnp.mean(values * values, axis=-1, keepdims=True) + 1e-06)
    return jax.nn.gelu(values * scale * gain).astype(jnp.bfloat16)


def neighbours(hidden):
    return with_halo(hidden, (("seq", 1),), 2)


def plain(inputs, weights, gains):
    share = weights.shape[3]
    begin = lax.axis_index("section") * share
    hidden = normed(inputs, gains[0])
    conv = convolve(neighbours(hidden), weights[0])
    own = lax.dynamic_slice_in_dim(inputs, begin, share, 2)
    current = (own.astype(jnp.float32) + conv).astype(jnp.bfloat16)
    results = [current]
    kernel = weights[1]
    whole = lax.all_gather(current, "section", axis=2, tiled=True)
    conv = convolve(neighbours(normed(whole, gains[1])), kernel)
    current = (current.astype(jnp.float32) + conv).astype(jnp.bfloat16)
    results.append(current)
    return jnp.stack(results, axis=0)


def gelu_of_twice(h):
    return h + h * jnp.tanh(h * (1.5957691216057308 + 0.285419265090401 * (h * h)))


def chunk_ends(rows):
    tiles = rows // 16
    return [tiles * 11 // 32 * 16, tiles * 23 // 32 * 16, rows + 8]


def schedule(count):
    early = {5 + 2 * m: m for m in range(3)}
    between = list(range(len(early), min(len(early) + 2, count)))
    rest = range(len(early) + len(between), count)
    late = {}
    for n, m in enumerate(rest):
        late.setdefault(max(0, min(2 * n + 1, m - 1)), []).append(m)
    return early, between, late


def fused_kernel(
    x, w, g, out, xe, hid_a, hid_b, hid_c, hid1, y, yx, wv, wx, gv, acts, last,
    gsem, wsem, xsem, hsend, hrecv, ssem, rsem, osem, lsem,
    tsend, trecv, zsend, zrecv, psend, precv,
):
    micro, rows, chans = x.shape
    taps, share = w.shape[1], w.shape[3]
    span = rows + 2 * HALO
    ends = chunk_ends(rows)
    begins = [0] + ends[:-1]
    parts = len(ends)
    count = parts * micro
    me, seq = lax.axis_index("section"), lax.axis_index("seq")
    nseq = lax.axis_size("seq")
    planes = nseq // 2
    plane, core = seq // 2, seq % 2
    partner = seq + 1 - 2 * core
    piece_rows = chans // nseq
    early, between, late = schedule(count)

    def ring(at):
        r = at // 2
        return 2 * r + (at % 2) * (1 - 2 * (r % 2)) + r % 2

    place = ring(me)
    right, left = ring((place + 1) % 4), ring((place + 3) % 4)
    over = ring((place + 2) % 4)

    gains = pltpu.make_async_copy(g, gv, gsem)

    def load(b):
        return pltpu.make_async_copy(x.at[b], xe.at[b, pl.ds(HALO, rows)], xsem.at[b])

    def weight(l, k):
        return pltpu.make_async_copy(w.at[l, k], wv.at[l, :, pl.ds(k * share, share)], wsem.at[l, k])

    def load_part(n):
        part = ((0, ends[0] + 64), (ends[0] + 64, rows))[n]
        size = part[1] - part[0]
        return pltpu.make_async_copy(
            x.at[0, pl.ds(part[0], size)], xe.at[0, pl.ds(HALO + part[0], size)], xsem.at[n * micro]
        )

    gains.start()
    load_part(0).start()
    for k in range(taps):
        weight(0, k).start()
    load_part(1).start()

    barrier = pltpu.get_barrier_semaphore()
    for to in (right, left):
        pl.semaphore_signal(barrier, inc=1, device_id=(to, seq), device_id_type=MESH)

    def greet(reach):
        @pl.when(seq >= reach)
        def _():
            pl.semaphore_signal(barrier, inc=1, device_id=(me, seq - reach), device_id_type=MESH)

        @pl.when(seq < nseq - reach)
        def _():
            pl.semaphore_signal(barrier, inc=1, device_id=(me, seq + reach), device_id_type=MESH)

    greet(1)
    greet(2)
    peers = 2
    for reach in (1, 2):
        peers = peers + jnp.where(seq >= reach, 1, 0) + jnp.where(seq < nseq - reach, 1, 0)
    def halo_up(b):
        return pltpu.make_async_remote_copy(
            src_ref=x.at[b, pl.ds(rows - HALO, HALO), :],
            dst_ref=xe.at[b, pl.ds(0, HALO), :],
            send_sem=hsend.at[0, b],
            recv_sem=hrecv.at[0, b],
            device_id=(me, seq + 1),
            device_id_type=MESH,
        )

    def halo_down(b):
        return pltpu.make_async_remote_copy(
            src_ref=x.at[b, pl.ds(0, HALO), :],
            dst_ref=xe.at[b, pl.ds(HALO + rows, HALO), :],
            send_sem=hsend.at[1, b],
            recv_sem=hrecv.at[1, b],
            device_id=(me, seq - 1),
            device_id_type=MESH,
        )

    def tap(k):
        return pltpu.make_async_remote_copy(
            src_ref=w.at[0, k, pl.ds(seq * piece_rows, piece_rows), pl.ds(0, EXTRA)],
            dst_ref=wx.at[pl.ds(seq * piece_rows, piece_rows), pl.ds(k * EXTRA, EXTRA)],
            send_sem=tsend.at[k],
            recv_sem=trecv.at[k],
            device_id=(right, seq),
            device_id_type=MESH,
        )

    groups = ((0, 3), (3, taps))

    def block(index, n):
        low, high = groups[n]
        return wx.at[
            pl.ds(pl.multiple_of(index * piece_rows, 8), piece_rows),
            pl.ds(low * EXTRA, (high - low) * EXTRA),
        ]

    def spread(at, n, way, to):
        source = 2 * at + core
        return pltpu.make_async_remote_copy(
            src_ref=block(source, n),
            dst_ref=block(source, n),
            send_sem=zsend.at[way, at, n],
            recv_sem=zrecv.at[at, n],
            device_id=(me, to),
            device_id_type=MESH,
        )

    def swap(at, n):
        source = 2 * at + core
        return pltpu.make_async_remote_copy(
            src_ref=block(source, n),
            dst_ref=block(source, n),
            send_sem=psend.at[at, n],
            recv_sem=precv.at[at, n],
            device_id=(me, partner),
            device_id_type=MESH,
        )

    def swapped(at, n):
        source = 2 * at + 1 - core
        return pltpu.make_async_remote_copy(
            src_ref=block(source, n),
            dst_ref=block(source, n),
            send_sem=psend.at[at, n],
            recv_sem=precv.at[at, n],
            device_id=(me, partner),
            device_id_type=MESH,
        )

    def spread_own(n):
        for k in range(*groups[n]):
            tap(k).wait_recv()

        @pl.when(plane < planes - 1)
        def _():
            spread(plane, n, 0, seq + 2).start()

        @pl.when(plane > 0)
        def _():
            spread(plane, n, 1, seq - 2).start()

        swap(plane, n).start()

    def spread_far(d, n):
        @pl.when(plane >= d)
        def _():
            spread(plane - d, n, 0, seq).wait_recv()

            @pl.when(plane < planes - 1)
            def _():
                spread(plane - d, n, 0, seq + 2).start()

            swap(plane - d, n).start()

        @pl.when(plane < planes - d)
        def _():
            spread(plane + d, n, 1, seq).wait_recv()

            @pl.when(plane > 0)
            def _():
                spread(plane + d, n, 1, seq - 2).start()

            swap(plane + d, n).start()

    def spread_sent():
        for n in range(len(groups)):
            for k in range(*groups[n]):
                tap(k).wait_send()
            for at in range(planes):
                swap(at, n).wait_send()

                @pl.when((plane >= at) & (plane < planes - 1))
                def _():
                    spread(at, n, 0, seq + 2).wait_send()

                @pl.when((plane <= at) & (plane > 0))
                def _():
                    spread(at, n, 1, seq - 2).wait_send()

    @pl.when(seq == 0)
    def _():
        xe[:, 0:HALO, :] = jnp.zeros((micro, HALO, chans), jnp.bfloat16)

    @pl.when(seq == nseq - 1)
    def _():
        xe[:, HALO + rows : span, :] = jnp.zeros((micro, HALO, chans), jnp.bfloat16)

    def enter():
        pl.semaphore_wait(barrier, peers)
        for k in range(taps):
            tap(k).start()

        @pl.when(seq < nseq - 1)
        def _():
            for b in range(micro):
                halo_up(b).start()

        @pl.when(seq > 0)
        def _():
            for b in range(micro):
                halo_down(b).start()

    def send(origin, c, way, to):
        b, t = c // parts, c % parts
        size = ends[t] - begins[t]
        low, high = ((EXTRA, share), (0, share), (EXTRA, share), (0, EXTRA))[way]
        ref = acts.at[origin, b, pl.ds(begins[t], size), pl.ds(low, high - low)]
        return pltpu.make_async_remote_copy(
            src_ref=ref,
            dst_ref=ref,
            send_sem=ssem.at[way, c],
            recv_sem=rsem.at[way, c],
            device_id=(to, seq),
            device_id_type=MESH,
        )

    def direct(c):
        send(me, c, 0, right).start()
        send(me, c, 1, left).start()

    def forward(c):
        send(left, c, 0, left).wait_recv()
        send(left, c, 2, right).start()
        send(right, c, 1, right).wait_recv()
        send(right, c, 3, left).start()
        if c + 3 < count:
            direct(c + 3)

    def arrived(b, t):
        size = ends[t] - begins[t]
        c = b * parts + t
        for way, low, high in ((2, EXTRA, share), (3, 0, EXTRA)):
            ref = acts.at[over, b, pl.ds(begins[t], size), pl.ds(low, high - low)]
            pltpu.make_async_remote_copy(
                src_ref=ref,
                dst_ref=ref,
                send_sem=ssem.at[way, c],
                recv_sem=rsem.at[way, c],
                device_id=(right, seq),
                device_id_type=MESH,
            ).wait_recv()

    tile = 16

    def activate(v, l):
        scale = lax.rsqrt(jnp.mean(v * v, axis=-1, keepdims=True) + 1e-06)
        return gelu_of_twice(v * (0.5 * scale) * gv[l : l + 1, :]).astype(jnp.bfloat16)

    step = 512

    def product(dst, src, kernel, begin, end, wide, which=slice(None), beside=()):
        starts = list(range(0, wide, step))[which]
        for i, n in enumerate(starts):
            for tile_work in beside[i :: len(starts)]:
                tile_work()
            size = min(step, wide - n)
            dst[begin + 8 : end + 8, n : n + size] = jnp.dot(
                src(begin, end), kernel(n, size), preferred_element_type=jnp.float32
            )

    def close(dst):
        dst[0:8, :] = dst[rows + 16 : rows + 24, :]
        dst[rows + 24 : rows + 32, :] = dst[8:16, :]

    def gather_taps(src, u, width, stride):
        total = None
        block = src[u : u + tile + 16, :]
        for k in range(taps):
            term = block[8 - REACH + k : 8 - REACH + k + tile, k * stride : k * stride + width]
            total = term if total is None else total + term
        return total

    mine = pl.ds(pl.multiple_of(me * share, 128), share)
    theirs = pl.ds(pl.multiple_of(left * share, 128), EXTRA)

    def source(b, u, columns):
        if u == rows - 16:
            bottom = xe[b, HALO + rows : span, columns].astype(jnp.float32)
            top = xe[b, 0:HALO, columns].astype(jnp.float32)
            return jnp.concatenate([bottom[0:8, :], top[8:16, :]], axis=0)
        at = HALO if u == rows else 2 * HALO + u
        return xe[b, at : at + tile, columns].astype(jnp.float32)

    edges0 = [0] + [e + 2 * tile for e in ends[:-1]] + [rows + 16]

    hid = (hid_a, hid_b, hid_c)

    def norm_first(b, t):
        def work(u):
            at = u - edges0[t]
            hid[t][b, at : at + tile, :] = activate(source(b, u, slice(None)), 0)

        return [functools.partial(work, u) for u in range(edges0[t], edges0[t + 1], tile)]

    def outputs(edges, t):
        begin = tile if t == 0 else edges[t] - tile
        end = edges[t + 1] if t == parts - 1 else edges[t + 1] - tile
        return list(range(begin, end, tile)) + ([0] if t == parts - 1 else [])

    def conv_first(b, t, src, owner, columns, width, stride):
        for u in outputs(edges0, t):
            value = source(b, u, columns) + gather_taps(src, u, width, stride)
            at = u - tile
            if u == rows - 16:
                at = rows
                row = lax.broadcasted_iota(jnp.int32, (8, width), 0)
                value = jnp.where(row < 4, value[0:8, :], value[8:16, :])
                inside = ((row < 4) & (seq < nseq - 1)) | ((row >= 4) & (seq > 0))
                value = jnp.where(inside, value, 0.0)
                value = jnp.concatenate([value, jnp.zeros_like(value)], axis=0)
            elif u == rows:
                at = rows - 32
            elif u == 0:
                at = rows - 16
            acts[owner, b, at : at + tile, 0:width] = value.astype(jnp.bfloat16)

    def multiply_first(b, t, which, beside=()):
        product(
            y, lambda p, q: hid[t][b], lambda n, s: wv[0, :, n : n + s],
            edges0[t], edges0[t + 1], taps * share, which, beside,
        )

    def finish_first(b, t):
        if t == parts - 1:
            close(y)
        conv_first(b, t, y, me, mine, share, share)

    head, tail = slice(0, 1), slice(1, None)

    def extra(b, t, which, beside=()):
        product(
            yx, lambda p, q: hid[t][b], lambda n, s: wx[:, n : n + s],
            edges0[t], edges0[t + 1], taps * EXTRA, which, beside,
        )

    def finish_extra(b, t):
        if t == parts - 1:
            close(yx)
        conv_first(b, t, yx, left, theirs, EXTRA, EXTRA)

    edges1 = [0] + ends[:-1] + [rows + 16]

    def held(u):
        return u if u < rows - 32 else rows if u == rows - 32 else u - 16

    def norm_second(b, t):
        def work(u):
            at = held(u)
            pieces = [acts[s, b, at : at + tile, :].astype(jnp.float32) for s in range(4)]
            value = jnp.concatenate(pieces, axis=-1)
            if at == rows:
                value = jnp.concatenate([value[0:8, :], value[0:8, :]], axis=0)
            hid1[u : u + tile, :] = activate(value, 1)

        return [functools.partial(work, u) for u in range(edges1[t], edges1[t + 1], tile)]

    def multiply_second(b, t, beside=()):
        product(
            y, lambda p, q: hid1[p:q, :], lambda n, s: wv[1, :, n : n + s],
            edges1[t], edges1[t + 1], taps * share, beside=beside,
        )

    def finish_second(b, t):
        if t == parts - 1:
            close(y)
        for u in outputs(edges1, t):
            if u == rows - 32:
                continue
            at = held(u)
            value = acts[me, b, at : at + tile, :].astype(jnp.float32)
            value = value + gather_taps(y, u, share, share)
            row = u + 32 if u < rows - 32 else u - (rows - 16)
            last[b, row : row + tile, :] = value.astype(jnp.bfloat16)

    def out_first(b, n):
        begin, size, row = ((0, rows - 32, 32), (rows - 32, 32, 0))[n]
        return pltpu.make_async_copy(
            acts.at[me, b, pl.ds(begin, size), :], out.at[0, b, pl.ds(row, size)], osem.at[b, n]
        )

    cuts = (0, 32 + tile, edges1[-2] + 32 - tile, rows)

    def out_last(b, n):
        part = pl.ds(cuts[n], cuts[n + 1] - cuts[n])
        return pltpu.make_async_copy(last.at[b, part], out.at[1, b, part], lsem.at[b, n])

    def at_step(b, t, table, act):
        for bb in range(micro):
            for m in table.get(bb * parts + t, ()):
                pl.when(b == bb)(lambda m=m: act(m))

    errands = {}
    for n in range(len(groups)):
        errands.setdefault(2 + n, []).append(("own", 0, n))
        for d in range(1, planes):
            errands.setdefault(min(2 + 3 * d + n, count), []).append(("far", d, n))

    def errand(e):
        kind, d, n = e
        if kind == "own":
            spread_own(n)
        else:
            spread_far(d, n)

    gains.wait()
    load_part(0).wait()
    for work in norm_first(0, 0):
        work()
    enter()
    for k in range(2):
        weight(0, k).wait()
    multiply_first(0, 0, head)
    for other in range(1, micro):
        load(other).start()
    for k in range(taps):
        weight(1, k).start()
    for k in range(2, taps):
        weight(0, k).wait()
    load_part(1).wait()

    @pl.loop(0, micro)
    def _(b):
        for t in range(parts):
            if t == 1:

                @pl.when(seq > 0)
                def _():
                    halo_up(b).wait_recv()

                @pl.when(seq < nseq - 1)
                def _():
                    halo_down(b).wait_recv()

            if t < parts - 1:
                multiply_first(b, t, tail, norm_first(b, t + 1))
                finish_first(b, t)
                multiply_first(b, t + 1, head)
            else:

                @pl.when(b < micro - 1)
                def _():
                    load(b + 1).wait()
                    multiply_first(b, t, tail, norm_first(b + 1, 0))
                    finish_first(b, t)
                    multiply_first(b + 1, 0, head)

                @pl.when(b == micro - 1)
                def _():
                    multiply_first(b, t, tail)
                    finish_first(b, t)

            at_step(b, t, {c: (c,) for c in range(3)}, direct)
            at_step(b, t, {p: (m,) for p, m in early.items()}, forward)
            at_step(b, t, errands, errand)
        for n in range(2):
            out_first(b, n).start()

    for m in between[:1]:
        forward(m)
    for e in errands.get(count, ()):
        errand(e)
    for n in range(len(groups)):
        for at in range(planes):
            swapped(at, n).wait_recv()
    for m in between[1:]:
        forward(m)
    extra(0, 0, slice(None))
    finish_extra(0, 0)
    for k in range(taps):
        weight(1, k).wait()

    @pl.loop(0, micro)
    def _(b):
        for t in range(parts):
            at_step(b, t, late, forward)
            arrived(b, t)
            if t < parts - 1:
                extra(b, t + 1, head, norm_second(b, t))
                multiply_second(b, t)
                extra(b, t + 1, tail)
                finish_second(b, t)
                finish_extra(b, t + 1)
            else:

                @pl.when(b < micro - 1)
                def _():
                    extra(b + 1, 0, head, norm_second(b, t))
                    multiply_second(b, t)
                    extra(b + 1, 0, tail)
                    finish_second(b, t)
                    finish_extra(b + 1, 0)

                @pl.when(b == micro - 1)
                def _():
                    for work in norm_second(b, t):
                        work()
                    multiply_second(b, t)
                    finish_second(b, t)

            if t == parts - 2:
                out_last(b, 1).start()
        out_last(b, 0).start()
        out_last(b, 2).start()

    @pl.when(seq < nseq - 1)
    def _():
        for b in range(micro):
            halo_up(b).wait_send()

    @pl.when(seq > 0)
    def _():
        for b in range(micro):
            halo_down(b).wait_send()

    spread_sent()
    for c in range(count):
        send(me, c, 0, right).wait_send()
        send(me, c, 1, left).wait_send()
        send(left, c, 2, right).wait_send()
        send(right, c, 3, left).wait_send()

    @pl.loop(0, micro)
    def _(b):
        for n in range(2):
            out_first(b, n).wait()
        for n in range(3):
            out_last(b, n).wait()


def fused(inputs, weights, gains):
    micro, rows, chans = inputs.shape
    layers, taps, _, share = weights.shape
    span = rows + 2 * HALO
    count = len(chunk_ends(rows)) * micro
    ends = chunk_ends(rows)
    edges = [0] + [e + 32 for e in ends[:-1]] + [rows + 16]
    sizes = [q - p for p, q in zip(edges, edges[1:])]
    planes = lax.axis_size("seq") // 2
    dma = pltpu.SemaphoreType.DMA
    hbm = pl.BlockSpec(memory_space=pltpu.HBM)
    return pl.pallas_call(
        fused_kernel,
        out_shape=jax.ShapeDtypeStruct((layers, micro, rows, share), jnp.bfloat16),
        in_specs=[hbm, hbm, hbm],
        out_specs=pl.BlockSpec(memory_space=pl.ANY),
        scratch_shapes=[
            pltpu.VMEM((micro, span, chans), jnp.bfloat16),
            *(pltpu.VMEM((micro, n, chans), jnp.bfloat16) for n in sizes),
            pltpu.VMEM((rows + HALO, chans), jnp.bfloat16),
            pltpu.VMEM((rows + 32, taps * share), jnp.float32),
            pltpu.VMEM((rows + 32, taps * EXTRA), jnp.float32),
            pltpu.VMEM((2, chans, taps * share), jnp.bfloat16),
            pltpu.VMEM((chans, taps * EXTRA), jnp.bfloat16),
            pltpu.VMEM(gains.shape, jnp.float32),
            pltpu.VMEM((4, micro, rows + HALO, share), jnp.bfloat16),
            pltpu.VMEM((micro, rows, share), jnp.bfloat16),
            dma,
            dma((2, taps)),
            dma((micro + 1,)),
            dma((2, micro)),
            dma((2, micro)),
            dma((4, count)),
            dma((4, count)),
            dma((micro, 2)),
            dma((micro, 3)),
            dma((taps,)),
            dma((taps,)),
            dma((2, planes, 2)),
            dma((planes, 2)),
            dma((planes, 2)),
            dma((planes, 2)),
        ],
        compiler_params=pltpu.CompilerParams(
            collective_id=0, has_side_effects=True, vmem_limit_bytes=50 * 1024 * 1024
        ),
    )(inputs, weights, gains)


def local(inputs, weights, gains):
    micro, rows, chans = inputs.shape
    layers, taps, _, share = weights.shape
    nseq = lax.axis_size("seq")
    square = lax.axis_size("section") == 4 and layers == 2 and nseq % 2 == 0 and nseq > 2
    wide = share % 128 == 0 and share > EXTRA and chans % (16 * nseq) == 0
    if square and wide and taps == 5 and micro > 1 and rows % 512 == 0:
        return fused(inputs, weights, gains)
    return plain(inputs, weights, gains)


def solution(mesh):
    in_specs = (P(None, "seq", None), P(None, None, None, "section"), P())
    out_specs = P(None, None, "seq", "section")
    return jax.shard_map(local, mesh=mesh, in_specs=in_specs, out_specs=out_specs, check_vma=False)
```

```python
import functools
import jax
import jax.numpy as jnp
from jax import lax
from jax.experimental import pallas as pl
from jax.experimental.pallas import tpu as pltpu
from jax.sharding import PartitionSpec as P

MESH = pl.DeviceIdType.MESH
HALO = 16
REACH = 2
EXTRA = 128


def with_halo(value, sides, width):
    for axis, dim in sides:
        count, length = (lax.axis_size(axis), value.shape[dim])
        up = [(i, (i + 1) % count) for i in range(count - 1)]
        down = [(j, i) for i, j in up]
        last = lax.slice_in_dim(value, length - width, length, axis=dim)
        initial = lax.slice_in_dim(value, 0, width, axis=dim)
        before = lax.ppermute(last, axis, up)
        after = lax.ppermute(initial, axis, down)
        value = jnp.concatenate([before, value, after], axis=dim)
    return value


def convolve(padded, kernel):
    count = padded.shape[1] - 4
    total = jnp.zeros((padded.shape[0], count, kernel.shape[2]), jnp.float32)
    for k in range(5):
        total = total + jnp.einsum(
            "brc,co->bro", padded[:, k : k + count], kernel[k], preferred_element_type=jnp.float32
        )
    return total


def normed(current, gain):
    values = current.astype(jnp.float32)
    scale = lax.rsqrt(jnp.mean(values * values, axis=-1, keepdims=True) + 1e-06)
    return jax.nn.gelu(values * scale * gain).astype(jnp.bfloat16)


def neighbours(hidden):
    return with_halo(hidden, (("seq", 1),), 2)


def plain(inputs, weights, gains):
    share = weights.shape[3]
    begin = lax.axis_index("section") * share
    hidden = normed(inputs, gains[0])
    conv = convolve(neighbours(hidden), weights[0])
    own = lax.dynamic_slice_in_dim(inputs, begin, share, 2)
    current = (own.astype(jnp.float32) + conv).astype(jnp.bfloat16)
    results = [current]
    kernel = weights[1]
    whole = lax.all_gather(current, "section", axis=2, tiled=True)
    conv = convolve(neighbours(normed(whole, gains[1])), kernel)
    current = (current.astype(jnp.float32) + conv).astype(jnp.bfloat16)
    results.append(current)
    return jnp.stack(results, axis=0)


def gelu_of_twice(h):
    return h + h * jnp.tanh(h * (1.5957691216057308 + 0.285419265090401 * (h * h)))


def chunk_ends(rows):
    tiles = rows // 16
    return [tiles * 11 // 32 * 16, tiles * 23 // 32 * 16, rows + 8]


def schedule(count):
    early = {5 + 2 * m: m for m in range(3)}
    between = [len(early)]
    late = {m - 2: (m,) for m in range(len(early) + 1, count)}
    return early, between, late


def fused_kernel(
    x, w, g, out, xe, hid_a, hid_b, hid_c, hid1, y, yx, wv, wx, gv, acts, last,
    gsem, wsem, xsem, hsend, hrecv, ssem, rsem, osem, lsem,
    tsend, trecv, zsend, zrecv, psend, precv,
):
    micro, rows, chans = x.shape
    taps, share = w.shape[1], w.shape[3]
    span = rows + 2 * HALO
    ends = chunk_ends(rows)
    begins = [0] + ends[:-1]
    parts = len(ends)
    count = parts * micro
    me, seq = lax.axis_index("section"), lax.axis_index("seq")
    nseq = lax.axis_size("seq")
    planes = nseq // 2
    plane, core = seq // 2, seq % 2
    partner = seq + 1 - 2 * core
    piece_rows = chans // nseq
    early, between, late = schedule(count)

    def ring(at):
        r = at // 2
        return 2 * r + (at % 2) * (1 - 2 * (r % 2)) + r % 2

    place = ring(me)
    right, left = ring((place + 1) % 4), ring((place + 3) % 4)
    over = ring((place + 2) % 4)

    gains = pltpu.make_async_copy(g, gv, gsem)

    def load(b):
        return pltpu.make_async_copy(x.at[b], xe.at[b, pl.ds(HALO, rows)], xsem.at[b])

    def weight(l, k):
        return pltpu.make_async_copy(w.at[l, k], wv.at[l, :, pl.ds(k * share, share)], wsem.at[l, k])

    def load_part(n):
        part = ((0, ends[0] + 64), (ends[0] + 64, rows))[n]
        size = part[1] - part[0]
        return pltpu.make_async_copy(
            x.at[0, pl.ds(part[0], size)], xe.at[0, pl.ds(HALO + part[0], size)], xsem.at[n * micro]
        )

    gains.start()
    load_part(0).start()
    for k in range(taps):
        weight(0, k).start()
    load_part(1).start()

    barrier = pltpu.get_barrier_semaphore()
    for to in (right, left):
        pl.semaphore_signal(barrier, inc=1, device_id=(to, seq), device_id_type=MESH)

    def greet(reach):
        @pl.when(seq >= reach)
        def _():
            pl.semaphore_signal(barrier, inc=1, device_id=(me, seq - reach), device_id_type=MESH)

        @pl.when(seq < nseq - reach)
        def _():
            pl.semaphore_signal(barrier, inc=1, device_id=(me, seq + reach), device_id_type=MESH)

    greet(1)
    greet(2)
    peers = 2
    for reach in (1, 2):
        peers = peers + jnp.where(seq >= reach, 1, 0) + jnp.where(seq < nseq - reach, 1, 0)
    def halo_up(b):
        return pltpu.make_async_remote_copy(
            src_ref=x.at[b, pl.ds(rows - HALO, HALO), :],
            dst_ref=xe.at[b, pl.ds(0, HALO), :],
            send_sem=hsend.at[0, b],
            recv_sem=hrecv.at[0, b],
            device_id=(me, seq + 1),
            device_id_type=MESH,
        )

    def halo_down(b):
        return pltpu.make_async_remote_copy(
            src_ref=x.at[b, pl.ds(0, HALO), :],
            dst_ref=xe.at[b, pl.ds(HALO + rows, HALO), :],
            send_sem=hsend.at[1, b],
            recv_sem=hrecv.at[1, b],
            device_id=(me, seq - 1),
            device_id_type=MESH,
        )

    def tap(k):
        return pltpu.make_async_remote_copy(
            src_ref=w.at[0, k, pl.ds(seq * piece_rows, piece_rows), pl.ds(0, EXTRA)],
            dst_ref=wx.at[pl.ds(seq * piece_rows, piece_rows), pl.ds(k * EXTRA, EXTRA)],
            send_sem=tsend.at[k],
            recv_sem=trecv.at[k],
            device_id=(right, seq),
            device_id_type=MESH,
        )

    groups = ((0, 3), (3, taps))

    def block(index, n):
        low, high = groups[n]
        return wx.at[
            pl.ds(pl.multiple_of(index * piece_rows, 8), piece_rows),
            pl.ds(low * EXTRA, (high - low) * EXTRA),
        ]

    def spread(at, n, way, to):
        source = 2 * at + core
        return pltpu.make_async_remote_copy(
            src_ref=block(source, n),
            dst_ref=block(source, n),
            send_sem=zsend.at[way, at, n],
            recv_sem=zrecv.at[at, n],
            device_id=(me, to),
            device_id_type=MESH,
        )

    def swap(at, n):
        source = 2 * at + core
        return pltpu.make_async_remote_copy(
            src_ref=block(source, n),
            dst_ref=block(source, n),
            send_sem=psend.at[at, n],
            recv_sem=precv.at[at, n],
            device_id=(me, partner),
            device_id_type=MESH,
        )

    def swapped(at, n):
        source = 2 * at + 1 - core
        return pltpu.make_async_remote_copy(
            src_ref=block(source, n),
            dst_ref=block(source, n),
            send_sem=psend.at[at, n],
            recv_sem=precv.at[at, n],
            device_id=(me, partner),
            device_id_type=MESH,
        )

    def spread_own(n):
        for k in range(*groups[n]):
            tap(k).wait_recv()

        @pl.when(plane < planes - 1)
        def _():
            spread(plane, n, 0, seq + 2).start()

        @pl.when(plane > 0)
        def _():
            spread(plane, n, 1, seq - 2).start()

        swap(plane, n).start()

    def spread_far(d, n):
        @pl.when(plane >= d)
        def _():
            spread(plane - d, n, 0, seq).wait_recv()

            @pl.when(plane < planes - 1)
            def _():
                spread(plane - d, n, 0, seq + 2).start()

            swap(plane - d, n).start()

        @pl.when(plane < planes - d)
        def _():
            spread(plane + d, n, 1, seq).wait_recv()

            @pl.when(plane > 0)
            def _():
                spread(plane + d, n, 1, seq - 2).start()

            swap(plane + d, n).start()

    def spread_sent():
        for n in range(len(groups)):
            for k in range(*groups[n]):
                tap(k).wait_send()
            for at in range(planes):
                swap(at, n).wait_send()

                @pl.when((plane >= at) & (plane < planes - 1))
                def _():
                    spread(at, n, 0, seq + 2).wait_send()

                @pl.when((plane <= at) & (plane > 0))
                def _():
                    spread(at, n, 1, seq - 2).wait_send()

    @pl.when(seq == 0)
    def _():
        xe[:, 0:HALO, :] = jnp.zeros((micro, HALO, chans), jnp.bfloat16)

    @pl.when(seq == nseq - 1)
    def _():
        xe[:, HALO + rows : span, :] = jnp.zeros((micro, HALO, chans), jnp.bfloat16)

    def enter():
        pl.semaphore_wait(barrier, peers)
        for k in range(taps):
            tap(k).start()

        @pl.when(seq < nseq - 1)
        def _():
            for b in range(micro):
                halo_up(b).start()

        @pl.when(seq > 0)
        def _():
            for b in range(micro):
                halo_down(b).start()

    def channels(way, whole):
        if whole:
            return ((0, share), (0, share), (2 * EXTRA, share), (0, 2 * EXTRA))[way]
        return ((EXTRA, share), (0, share), (EXTRA, share), (0, EXTRA))[way]

    def send(origin, c, way, to):
        b, t = c // parts, c % parts
        size = ends[t] - begins[t]
        low, high = channels(way, b == 0)
        ref = acts.at[origin, b, pl.ds(begins[t], size), pl.ds(low, high - low)]
        return pltpu.make_async_remote_copy(
            src_ref=ref,
            dst_ref=ref,
            send_sem=ssem.at[way, c],
            recv_sem=rsem.at[way, c],
            device_id=(to, seq),
            device_id_type=MESH,
        )

    def direct(c):
        send(me, c, 0, right).start()
        send(me, c, 1, left).start()

    def forward(c):
        send(left, c, 0, left).wait_recv()
        send(left, c, 2, right).start()
        send(right, c, 1, right).wait_recv()
        send(right, c, 3, left).start()
        if c + 4 < count:
            direct(c + 4)

    def arrived(b, t):
        pl.when(b == 0)(lambda: arrived_in(b, t, True))
        pl.when(b > 0)(lambda: arrived_in(b, t, False))

    def arrived_in(b, t, whole):
        size = ends[t] - begins[t]
        c = b * parts + t
        for way in (2, 3):
            low, high = channels(way, whole)
            ref = acts.at[over, b, pl.ds(begins[t], size), pl.ds(low, high - low)]
            pltpu.make_async_remote_copy(
                src_ref=ref,
                dst_ref=ref,
                send_sem=ssem.at[way, c],
                recv_sem=rsem.at[way, c],
                device_id=(right, seq),
                device_id_type=MESH,
            ).wait_recv()

    tile = 16

    def activate(v, l):
        scale = lax.rsqrt(jnp.mean(v * v, axis=-1, keepdims=True) + 1e-06)
        return gelu_of_twice(v * (0.5 * scale) * gv[l : l + 1, :]).astype(jnp.bfloat16)

    step = 512

    def product(dst, src, kernel, begin, end, wide, which=slice(None), beside=()):
        starts = list(range(0, wide, step))[which]
        for i, n in enumerate(starts):
            for tile_work in beside[i :: len(starts)]:
                tile_work()
            size = min(step, wide - n)
            dst[begin + 8 : end + 8, n : n + size] = jnp.dot(
                src(begin, end), kernel(n, size), preferred_element_type=jnp.float32
            )

    def close(dst):
        dst[0:8, :] = dst[rows + 16 : rows + 24, :]
        dst[rows + 24 : rows + 32, :] = dst[8:16, :]

    def gather_taps(src, u, width, stride):
        total = None
        block = src[u : u + tile + 16, :]
        for k in range(taps):
            term = block[8 - REACH + k : 8 - REACH + k + tile, k * stride : k * stride + width]
            total = term if total is None else total + term
        return total

    mine = pl.ds(pl.multiple_of(me * share, 128), share)
    theirs = pl.ds(pl.multiple_of(left * share, 128), EXTRA)

    def source(b, u, columns):
        if u == rows - 16:
            bottom = xe[b, HALO + rows : span, columns].astype(jnp.float32)
            top = xe[b, 0:HALO, columns].astype(jnp.float32)
            return jnp.concatenate([bottom[0:8, :], top[8:16, :]], axis=0)
        at = HALO if u == rows else 2 * HALO + u
        return xe[b, at : at + tile, columns].astype(jnp.float32)

    edges0 = [0] + [e + 2 * tile for e in ends[:-1]] + [rows + 16]

    hid = (hid_a, hid_b, hid_c)

    def norm_first(b, t):
        def work(u):
            at = u - edges0[t]
            hid[t][b, at : at + tile, :] = activate(source(b, u, slice(None)), 0)

        return [functools.partial(work, u) for u in range(edges0[t], edges0[t + 1], tile)]

    def outputs(edges, t):
        begin = tile if t == 0 else edges[t] - tile
        end = edges[t + 1] if t == parts - 1 else edges[t + 1] - tile
        return list(range(begin, end, tile)) + ([0] if t == parts - 1 else [])

    def conv_first(b, t, src, owner, columns, width, stride):
        for u in outputs(edges0, t):
            value = source(b, u, columns) + gather_taps(src, u, width, stride)
            at = u - tile
            if u == rows - 16:
                at = rows
                row = lax.broadcasted_iota(jnp.int32, (8, width), 0)
                value = jnp.where(row < 4, value[0:8, :], value[8:16, :])
                inside = ((row < 4) & (seq < nseq - 1)) | ((row >= 4) & (seq > 0))
                value = jnp.where(inside, value, 0.0)
                value = jnp.concatenate([value, jnp.zeros_like(value)], axis=0)
            elif u == rows:
                at = rows - 32
            elif u == 0:
                at = rows - 16
            acts[owner, b, at : at + tile, 0:width] = value.astype(jnp.bfloat16)

    def multiply_first(b, t, which, beside=()):
        product(
            y, lambda p, q: hid[t][b], lambda n, s: wv[0, :, n : n + s],
            edges0[t], edges0[t + 1], taps * share, which, beside,
        )

    def finish_first(b, t):
        if t == parts - 1:
            close(y)
        conv_first(b, t, y, me, mine, share, share)

    head, tail = slice(0, 1), slice(1, None)

    def extra(b, t, which, beside=()):
        product(
            yx, lambda p, q: hid[t][b], lambda n, s: wx[:, n : n + s],
            edges0[t], edges0[t + 1], taps * EXTRA, which, beside,
        )

    def finish_extra(b, t):
        if t == parts - 1:
            close(yx)
        conv_first(b, t, yx, left, theirs, EXTRA, EXTRA)

    edges1 = [0] + ends[:-1] + [rows + 16]

    def held(u):
        return u if u < rows - 32 else rows if u == rows - 32 else u - 16

    def norm_second(b, t):
        def work(u):
            at = held(u)
            pieces = [acts[s, b, at : at + tile, :].astype(jnp.float32) for s in range(4)]
            value = jnp.concatenate(pieces, axis=-1)
            if at == rows:
                value = jnp.concatenate([value[0:8, :], value[0:8, :]], axis=0)
            hid1[u : u + tile, :] = activate(value, 1)

        return [functools.partial(work, u) for u in range(edges1[t], edges1[t + 1], tile)]

    def multiply_second(b, t, beside=()):
        product(
            y, lambda p, q: hid1[p:q, :], lambda n, s: wv[1, :, n : n + s],
            edges1[t], edges1[t + 1], taps * share, beside=beside,
        )

    def finish_second(b, t):
        if t == parts - 1:
            close(y)
        for u in outputs(edges1, t):
            if u == rows - 32:
                continue
            at = held(u)
            value = acts[me, b, at : at + tile, :].astype(jnp.float32)
            value = value + gather_taps(y, u, share, share)
            row = u + 32 if u < rows - 32 else u - (rows - 16)
            last[b, row : row + tile, :] = value.astype(jnp.bfloat16)

    def out_first(b, n):
        begin, size, row = ((0, rows - 32, 32), (rows - 32, 32, 0))[n]
        return pltpu.make_async_copy(
            acts.at[me, b, pl.ds(begin, size), :], out.at[0, b, pl.ds(row, size)], osem.at[b, n]
        )

    cuts = (0, 32 + tile, edges1[-2] + 32 - tile, rows)

    def out_last(b, n):
        part = pl.ds(cuts[n], cuts[n + 1] - cuts[n])
        return pltpu.make_async_copy(last.at[b, part], out.at[1, b, part], lsem.at[b, n])

    def swaps_done():
        for n in range(len(groups)):
            for at in range(planes):
                swapped(at, n).wait_recv()

    def at_step(b, t, table, act):
        for bb in range(micro):
            for m in table.get(bb * parts + t, ()):
                pl.when(b == bb)(lambda m=m: act(m))

    errands = {}
    for n in range(len(groups)):
        errands.setdefault(3 + n, []).append(("own", 0, n))
        for d in range(1, planes):
            errands.setdefault(min(3 + 3 * d + n, count), []).append(("far", d, n))

    def errand(e):
        kind, d, n = e
        if kind == "own":
            spread_own(n)
        else:
            spread_far(d, n)

    gains.wait()
    load_part(0).wait()
    for work in norm_first(0, 0):
        work()
    enter()
    for k in range(2):
        weight(0, k).wait()
    multiply_first(0, 0, head)
    for other in range(1, micro):
        load(other).start()
    for k in range(taps):
        weight(1, k).start()
    for k in range(2, taps):
        weight(0, k).wait()
    load_part(1).wait()

    @pl.loop(0, micro)
    def _(b):
        for t in range(parts):
            if t == 1:

                @pl.when(seq > 0)
                def _():
                    halo_up(b).wait_recv()

                @pl.when(seq < nseq - 1)
                def _():
                    halo_down(b).wait_recv()

            if t < parts - 1:
                multiply_first(b, t, tail, norm_first(b, t + 1))
                finish_first(b, t)
                multiply_first(b, t + 1, head)
            else:

                @pl.when(b < micro - 1)
                def _():
                    load(b + 1).wait()
                    multiply_first(b, t, tail, norm_first(b + 1, 0))
                    finish_first(b, t)
                    multiply_first(b + 1, 0, head)

                @pl.when(b == micro - 1)
                def _():
                    multiply_first(b, t, tail)
                    finish_first(b, t)

            at_step(b, t, {c: (c,) for c in range(4)}, direct)
            at_step(b, t, {p: (m,) for p, m in early.items()}, forward)
            at_step(b, t, errands, errand)
        for n in range(2):
            out_first(b, n).start()

    for m in between:
        forward(m)
    for k in range(taps):
        weight(1, k).wait()

    def step_second(b, t, more):
        norms = norm_second(b, t)
        for n in more:
            extra(b + 1, n, head, norms)
            norms = ()
            if n != more[-1]:
                extra(b + 1, n, tail)
                finish_extra(b + 1, n)
        for work in norms:
            work()
        multiply_second(b, t)
        if more:
            extra(b + 1, more[-1], tail)
        finish_second(b, t)
        if more:
            finish_extra(b + 1, more[-1])

    @pl.loop(0, micro)
    def _(b):
        for t in range(parts):
            at_step(b, t, late, forward)
            at_step(b, t, {1: errands.get(count, ())}, errand)
            at_step(b, t, {1: (0,)}, lambda _: swaps_done())
            arrived(b, t)
            if t == 0:
                pl.when((b > 0) & (b < micro - 1))(lambda: step_second(b, 0, (0,)))
                pl.when((b == 0) | (b == micro - 1))(lambda: step_second(b, 0, ()))
            elif t == 1:
                pl.when(b == 0)(lambda: step_second(b, 1, (0, 1)))
                pl.when((b > 0) & (b < micro - 1))(lambda: step_second(b, 1, (1,)))
                pl.when(b == micro - 1)(lambda: step_second(b, 1, ()))
            else:
                pl.when(b < micro - 1)(lambda: step_second(b, 2, (2,)))
                pl.when(b == micro - 1)(lambda: step_second(b, 2, ()))

            if t == parts - 2:
                out_last(b, 1).start()
        out_last(b, 0).start()
        out_last(b, 2).start()

    @pl.when(seq < nseq - 1)
    def _():
        for b in range(micro):
            halo_up(b).wait_send()

    @pl.when(seq > 0)
    def _():
        for b in range(micro):
            halo_down(b).wait_send()

    spread_sent()
    for c in range(count):
        send(me, c, 0, right).wait_send()
        send(me, c, 1, left).wait_send()
        send(left, c, 2, right).wait_send()
        send(right, c, 3, left).wait_send()

    @pl.loop(0, micro)
    def _(b):
        for n in range(2):
            out_first(b, n).wait()
        for n in range(3):
            out_last(b, n).wait()


def fused(inputs, weights, gains):
    micro, rows, chans = inputs.shape
    layers, taps, _, share = weights.shape
    span = rows + 2 * HALO
    count = len(chunk_ends(rows)) * micro
    ends = chunk_ends(rows)
    edges = [0] + [e + 32 for e in ends[:-1]] + [rows + 16]
    sizes = [q - p for p, q in zip(edges, edges[1:])]
    planes = lax.axis_size("seq") // 2
    dma = pltpu.SemaphoreType.DMA
    hbm = pl.BlockSpec(memory_space=pltpu.HBM)
    return pl.pallas_call(
        fused_kernel,
        out_shape=jax.ShapeDtypeStruct((layers, micro, rows, share), jnp.bfloat16),
        in_specs=[hbm, hbm, hbm],
        out_specs=pl.BlockSpec(memory_space=pl.ANY),
        scratch_shapes=[
            pltpu.VMEM((micro, span, chans), jnp.bfloat16),
            *(pltpu.VMEM((micro, n, chans), jnp.bfloat16) for n in sizes),
            pltpu.VMEM((rows + HALO, chans), jnp.bfloat16),
            pltpu.VMEM((rows + 32, taps * share), jnp.float32),
            pltpu.VMEM((rows + 32, taps * EXTRA), jnp.float32),
            pltpu.VMEM((2, chans, taps * share), jnp.bfloat16),
            pltpu.VMEM((chans, taps * EXTRA), jnp.bfloat16),
            pltpu.VMEM(gains.shape, jnp.float32),
            pltpu.VMEM((4, micro, rows + HALO, share), jnp.bfloat16),
            pltpu.VMEM((micro, rows, share), jnp.bfloat16),
            dma,
            dma((2, taps)),
            dma((micro + 1,)),
            dma((2, micro)),
            dma((2, micro)),
            dma((4, count)),
            dma((4, count)),
            dma((micro, 2)),
            dma((micro, 3)),
            dma((taps,)),
            dma((taps,)),
            dma((2, planes, 2)),
            dma((planes, 2)),
            dma((planes, 2)),
            dma((planes, 2)),
        ],
        compiler_params=pltpu.CompilerParams(
            collective_id=0, has_side_effects=True, vmem_limit_bytes=50 * 1024 * 1024
        ),
    )(inputs, weights, gains)


def local(inputs, weights, gains):
    micro, rows, chans = inputs.shape
    layers, taps, _, share = weights.shape
    nseq = lax.axis_size("seq")
    square = lax.axis_size("section") == 4 and layers == 2 and nseq % 2 == 0 and nseq > 2
    wide = share % 128 == 0 and share > 2 * EXTRA and chans % (16 * nseq) == 0
    if square and wide and taps == 5 and micro > 1 and rows % 512 == 0:
        return fused(inputs, weights, gains)
    return plain(inputs, weights, gains)


def solution(mesh):
    in_specs = (P(None, "seq", None), P(None, None, None, "section"), P())
    out_specs = P(None, None, "seq", "section")
    return jax.shard_map(local, mesh=mesh, in_specs=in_specs, out_specs=out_specs, check_vma=False)
```

```python
import functools
import jax
import jax.numpy as jnp
from jax import lax
from jax.experimental import pallas as pl
from jax.experimental.pallas import tpu as pltpu
from jax.sharding import PartitionSpec as P

MESH = pl.DeviceIdType.MESH
HALO = 16
REACH = 2
EXTRA = 128


def with_halo(value, sides, width):
    for axis, dim in sides:
        count, length = (lax.axis_size(axis), value.shape[dim])
        up = [(i, (i + 1) % count) for i in range(count - 1)]
        down = [(j, i) for i, j in up]
        last = lax.slice_in_dim(value, length - width, length, axis=dim)
        initial = lax.slice_in_dim(value, 0, width, axis=dim)
        before = lax.ppermute(last, axis, up)
        after = lax.ppermute(initial, axis, down)
        value = jnp.concatenate([before, value, after], axis=dim)
    return value


def convolve(padded, kernel):
    count = padded.shape[1] - 4
    total = jnp.zeros((padded.shape[0], count, kernel.shape[2]), jnp.float32)
    for k in range(5):
        total = total + jnp.einsum(
            "brc,co->bro", padded[:, k : k + count], kernel[k], preferred_element_type=jnp.float32
        )
    return total


def normed(current, gain):
    values = current.astype(jnp.float32)
    scale = lax.rsqrt(jnp.mean(values * values, axis=-1, keepdims=True) + 1e-06)
    return jax.nn.gelu(values * scale * gain).astype(jnp.bfloat16)


def neighbours(hidden):
    return with_halo(hidden, (("seq", 1),), 2)


def plain(inputs, weights, gains):
    share = weights.shape[3]
    begin = lax.axis_index("section") * share
    hidden = normed(inputs, gains[0])
    conv = convolve(neighbours(hidden), weights[0])
    own = lax.dynamic_slice_in_dim(inputs, begin, share, 2)
    current = (own.astype(jnp.float32) + conv).astype(jnp.bfloat16)
    results = [current]
    kernel = weights[1]
    whole = lax.all_gather(current, "section", axis=2, tiled=True)
    conv = convolve(neighbours(normed(whole, gains[1])), kernel)
    current = (current.astype(jnp.float32) + conv).astype(jnp.bfloat16)
    results.append(current)
    return jnp.stack(results, axis=0)


def gelu_of_twice(h):
    return h + h * jnp.tanh(h * (1.5957691216057308 + 0.285419265090401 * (h * h)))


def chunk_ends(rows):
    tiles = rows // 16
    return [tiles * 11 // 32 * 16, tiles * 23 // 32 * 16, rows + 8]


def schedule(count):
    early = {5 + 2 * m: m for m in range(3)}
    between = [len(early)]
    late = {m - 2: (m,) for m in range(len(early) + 1, count)}
    return early, between, late


def fused_kernel(
    x, w, g, out, xe, hid_a, hid_b, hid_c, hid1, y, yx, wv, wx, gv, acts,
    gsem, wsem, xsem, hsend, hrecv, ssem, rsem, osem,
    tsend, trecv, zsend, zrecv, psend, precv,
):
    micro, rows, chans = x.shape
    taps, share = w.shape[1], w.shape[3]
    span = rows + 2 * HALO
    ends = chunk_ends(rows)
    begins = [0] + ends[:-1]
    parts = len(ends)
    count = parts * micro
    me, seq = lax.axis_index("section"), lax.axis_index("seq")
    nseq = lax.axis_size("seq")
    planes = nseq // 2
    plane, core = seq // 2, seq % 2
    partner = seq + 1 - 2 * core
    piece_rows = chans // nseq
    early, between, late = schedule(count)

    def ring(at):
        r = at // 2
        return 2 * r + (at % 2) * (1 - 2 * (r % 2)) + r % 2

    place = ring(me)
    right, left = ring((place + 1) % 4), ring((place + 3) % 4)
    over = ring((place + 2) % 4)

    gains = pltpu.make_async_copy(g, gv, gsem)

    def load(b):
        return pltpu.make_async_copy(x.at[b], xe.at[b, pl.ds(HALO, rows)], xsem.at[b])

    def weight(l, k):
        return pltpu.make_async_copy(w.at[l, k], wv.at[l, :, pl.ds(k * share, share)], wsem.at[l, k])

    def load_part(n):
        part = ((0, ends[0] + 64), (ends[0] + 64, rows))[n]
        size = part[1] - part[0]
        return pltpu.make_async_copy(
            x.at[0, pl.ds(part[0], size)], xe.at[0, pl.ds(HALO + part[0], size)], xsem.at[n * micro]
        )

    gains.start()
    load_part(0).start()
    for k in range(taps):
        weight(0, k).start()
    load_part(1).start()

    barrier = pltpu.get_barrier_semaphore()
    for to in (right, left):
        pl.semaphore_signal(barrier, inc=1, device_id=(to, seq), device_id_type=MESH)

    def greet(reach):
        @pl.when(seq >= reach)
        def _():
            pl.semaphore_signal(barrier, inc=1, device_id=(me, seq - reach), device_id_type=MESH)

        @pl.when(seq < nseq - reach)
        def _():
            pl.semaphore_signal(barrier, inc=1, device_id=(me, seq + reach), device_id_type=MESH)

    greet(1)
    greet(2)
    peers = 2
    for reach in (1, 2):
        peers = peers + jnp.where(seq >= reach, 1, 0) + jnp.where(seq < nseq - reach, 1, 0)
    def halo_up(b):
        return pltpu.make_async_remote_copy(
            src_ref=x.at[b, pl.ds(rows - HALO, HALO), :],
            dst_ref=xe.at[b, pl.ds(0, HALO), :],
            send_sem=hsend.at[0, b],
            recv_sem=hrecv.at[0, b],
            device_id=(me, seq + 1),
            device_id_type=MESH,
        )

    def halo_down(b):
        return pltpu.make_async_remote_copy(
            src_ref=x.at[b, pl.ds(0, HALO), :],
            dst_ref=xe.at[b, pl.ds(HALO + rows, HALO), :],
            send_sem=hsend.at[1, b],
            recv_sem=hrecv.at[1, b],
            device_id=(me, seq - 1),
            device_id_type=MESH,
        )

    def tap(k):
        return pltpu.make_async_remote_copy(
            src_ref=w.at[0, k, pl.ds(seq * piece_rows, piece_rows), pl.ds(0, EXTRA)],
            dst_ref=wx.at[pl.ds(seq * piece_rows, piece_rows), pl.ds(k * EXTRA, EXTRA)],
            send_sem=tsend.at[k],
            recv_sem=trecv.at[k],
            device_id=(right, seq),
            device_id_type=MESH,
        )

    groups = ((0, 3), (3, taps))

    def block(index, n):
        low, high = groups[n]
        return wx.at[
            pl.ds(pl.multiple_of(index * piece_rows, 8), piece_rows),
            pl.ds(low * EXTRA, (high - low) * EXTRA),
        ]

    def spread(at, n, way, to):
        source = 2 * at + core
        return pltpu.make_async_remote_copy(
            src_ref=block(source, n),
            dst_ref=block(source, n),
            send_sem=zsend.at[way, at, n],
            recv_sem=zrecv.at[at, n],
            device_id=(me, to),
            device_id_type=MESH,
        )

    def swap(at, n):
        source = 2 * at + core
        return pltpu.make_async_remote_copy(
            src_ref=block(source, n),
            dst_ref=block(source, n),
            send_sem=psend.at[at, n],
            recv_sem=precv.at[at, n],
            device_id=(me, partner),
            device_id_type=MESH,
        )

    def swapped(at, n):
        source = 2 * at + 1 - core
        return pltpu.make_async_remote_copy(
            src_ref=block(source, n),
            dst_ref=block(source, n),
            send_sem=psend.at[at, n],
            recv_sem=precv.at[at, n],
            device_id=(me, partner),
            device_id_type=MESH,
        )

    def spread_own(n):
        for k in range(*groups[n]):
            tap(k).wait_recv()

        @pl.when(plane < planes - 1)
        def _():
            spread(plane, n, 0, seq + 2).start()

        @pl.when(plane > 0)
        def _():
            spread(plane, n, 1, seq - 2).start()

        swap(plane, n).start()

    def spread_far(d, n):
        @pl.when(plane >= d)
        def _():
            spread(plane - d, n, 0, seq).wait_recv()

            @pl.when(plane < planes - 1)
            def _():
                spread(plane - d, n, 0, seq + 2).start()

            swap(plane - d, n).start()

        @pl.when(plane < planes - d)
        def _():
            spread(plane + d, n, 1, seq).wait_recv()

            @pl.when(plane > 0)
            def _():
                spread(plane + d, n, 1, seq - 2).start()

            swap(plane + d, n).start()

    def spread_sent():
        for n in range(len(groups)):
            for k in range(*groups[n]):
                tap(k).wait_send()
            for at in range(planes):
                swap(at, n).wait_send()

                @pl.when((plane >= at) & (plane < planes - 1))
                def _():
                    spread(at, n, 0, seq + 2).wait_send()

                @pl.when((plane <= at) & (plane > 0))
                def _():
                    spread(at, n, 1, seq - 2).wait_send()

    @pl.when(seq == 0)
    def _():
        xe[:, 0:HALO, :] = jnp.zeros((micro, HALO, chans), jnp.bfloat16)

    @pl.when(seq == nseq - 1)
    def _():
        xe[:, HALO + rows : span, :] = jnp.zeros((micro, HALO, chans), jnp.bfloat16)

    def enter():
        pl.semaphore_wait(barrier, peers)
        for k in range(taps):
            tap(k).start()

        @pl.when(seq < nseq - 1)
        def _():
            for b in range(micro):
                halo_up(b).start()

        @pl.when(seq > 0)
        def _():
            for b in range(micro):
                halo_down(b).start()

    def channels(way, whole):
        if whole:
            return ((0, share), (0, share), (2 * EXTRA, share), (0, 2 * EXTRA))[way]
        return ((EXTRA, share), (0, share), (EXTRA, share), (0, EXTRA))[way]

    def send(origin, c, way, to):
        b, t = c // parts, c % parts
        size = ends[t] - begins[t]
        low, high = channels(way, b == 0)
        ref = acts.at[origin, b, pl.ds(begins[t], size), pl.ds(low, high - low)]
        return pltpu.make_async_remote_copy(
            src_ref=ref,
            dst_ref=ref,
            send_sem=ssem.at[way, c],
            recv_sem=rsem.at[way, c],
            device_id=(to, seq),
            device_id_type=MESH,
        )

    def direct(c):
        send(me, c, 0, right).start()
        send(me, c, 1, left).start()

    def forward(c):
        send(left, c, 0, left).wait_recv()
        send(left, c, 2, right).start()
        send(right, c, 1, right).wait_recv()
        send(right, c, 3, left).start()
        if c + 4 < count:
            direct(c + 4)

    def arrived(b, t):
        pl.when(b == 0)(lambda: arrived_in(b, t, True))
        pl.when(b > 0)(lambda: arrived_in(b, t, False))

    def arrived_in(b, t, whole):
        size = ends[t] - begins[t]
        c = b * parts + t
        for way in (2, 3):
            low, high = channels(way, whole)
            ref = acts.at[over, b, pl.ds(begins[t], size), pl.ds(low, high - low)]
            pltpu.make_async_remote_copy(
                src_ref=ref,
                dst_ref=ref,
                send_sem=ssem.at[way, c],
                recv_sem=rsem.at[way, c],
                device_id=(right, seq),
                device_id_type=MESH,
            ).wait_recv()

    tile = 16

    def activate(v, l):
        scale = lax.rsqrt(jnp.mean(v * v, axis=-1, keepdims=True) + 1e-06)
        return gelu_of_twice(v * (0.5 * scale) * gv[l : l + 1, :]).astype(jnp.bfloat16)

    step = 512

    def product(dst, src, kernel, begin, end, wide, which=slice(None), beside=()):
        starts = list(range(0, wide, step))[which]
        for i, n in enumerate(starts):
            for tile_work in beside[i :: len(starts)]:
                tile_work()
            size = min(step, wide - n)
            dst[begin + 8 : end + 8, n : n + size] = jnp.dot(
                src(begin, end), kernel(n, size), preferred_element_type=jnp.float32
            )

    def close(dst):
        dst[0:8, :] = dst[rows + 16 : rows + 24, :]
        dst[rows + 24 : rows + 32, :] = dst[8:16, :]

    def gather_taps(src, u, width, stride):
        total = None
        block = src[u : u + tile + 16, :]
        for k in range(taps):
            term = block[8 - REACH + k : 8 - REACH + k + tile, k * stride : k * stride + width]
            total = term if total is None else total + term
        return total

    mine = pl.ds(pl.multiple_of(me * share, 128), share)
    theirs = pl.ds(pl.multiple_of(left * share, 128), EXTRA)

    def source(b, u, columns):
        if u == rows - 16:
            bottom = xe[b, HALO + rows : span, columns].astype(jnp.float32)
            top = xe[b, 0:HALO, columns].astype(jnp.float32)
            return jnp.concatenate([bottom[0:8, :], top[8:16, :]], axis=0)
        at = HALO if u == rows else 2 * HALO + u
        return xe[b, at : at + tile, columns].astype(jnp.float32)

    edges0 = [0] + [e + 2 * tile for e in ends[:-1]] + [rows + 16]

    hid = (hid_a, hid_b, hid_c)

    def norm_first(b, t):
        def work(u):
            at = u - edges0[t]
            hid[t][b, at : at + tile, :] = activate(source(b, u, slice(None)), 0)

        return [functools.partial(work, u) for u in range(edges0[t], edges0[t + 1], tile)]

    def outputs(edges, t):
        begin = tile if t == 0 else edges[t] - tile
        end = edges[t + 1] if t == parts - 1 else edges[t + 1] - tile
        return list(range(begin, end, tile)) + ([0] if t == parts - 1 else [])

    def conv_first(b, t, src, owner, columns, width, stride):
        for u in outputs(edges0, t):
            value = source(b, u, columns) + gather_taps(src, u, width, stride)
            at = u - tile
            if u == rows - 16:
                at = rows
                row = lax.broadcasted_iota(jnp.int32, (8, width), 0)
                value = jnp.where(row < 4, value[0:8, :], value[8:16, :])
                inside = ((row < 4) & (seq < nseq - 1)) | ((row >= 4) & (seq > 0))
                value = jnp.where(inside, value, 0.0)
                value = jnp.concatenate([value, jnp.zeros_like(value)], axis=0)
            elif u == rows:
                at = rows - 32
            elif u == 0:
                at = rows - 16
            acts[owner, b, at : at + tile, 0:width] = value.astype(jnp.bfloat16)

    def multiply_first(b, t, which, beside=()):
        product(
            y, lambda p, q: hid[t][b], lambda n, s: wv[0, :, n : n + s],
            edges0[t], edges0[t + 1], taps * share, which, beside,
        )

    def finish_first(b, t):
        if t == parts - 1:
            close(y)
        conv_first(b, t, y, me, mine, share, share)

    head, tail = slice(0, 1), slice(1, None)

    def extra(b, t, which, beside=()):
        product(
            yx, lambda p, q: hid[t][b], lambda n, s: wx[:, n : n + s],
            edges0[t], edges0[t + 1], taps * EXTRA, which, beside,
        )

    def finish_extra(b, t):
        if t == parts - 1:
            close(yx)
        conv_first(b, t, yx, left, theirs, EXTRA, EXTRA)

    edges1 = [0] + ends[:-1] + [rows + 16]

    def held(u):
        return u if u < rows - 32 else rows if u == rows - 32 else u - 16

    def norm_second(b, t):
        def work(u):
            at = held(u)
            pieces = [acts[s, b, at : at + tile, :].astype(jnp.float32) for s in range(4)]
            value = jnp.concatenate(pieces, axis=-1)
            if at == rows:
                value = jnp.concatenate([value[0:8, :], value[0:8, :]], axis=0)
            hid1[u : u + tile, :] = activate(value, 1)

        return [functools.partial(work, u) for u in range(edges1[t], edges1[t + 1], tile)]

    def multiply_second(b, t, beside=()):
        product(
            y, lambda p, q: hid1[p:q, :], lambda n, s: wv[1, :, n : n + s],
            edges1[t], edges1[t + 1], taps * share, beside=beside,
        )

    def finish_second(b, t):
        if t == parts - 1:
            close(y)
        for u in outputs(edges1, t):
            if u == rows - 32:
                continue
            at = held(u)
            value = acts[me, b, at : at + tile, :].astype(jnp.float32)
            value = value + gather_taps(y, u, share, share)
            row = u + 32 if u < rows - 32 else u - (rows - 16)
            out[1, b, row : row + tile, :] = value.astype(jnp.bfloat16)

    def out_first(b, n):
        begin, size, row = ((0, rows - 32, 32), (rows - 32, 32, 0))[n]
        return pltpu.make_async_copy(
            acts.at[me, b, pl.ds(begin, size), :], out.at[0, b, pl.ds(row, size)], osem.at[b, n]
        )

    def swaps_done():
        for n in range(len(groups)):
            for at in range(planes):
                swapped(at, n).wait_recv()

    def at_step(b, t, table, act):
        for bb in range(micro):
            for m in table.get(bb * parts + t, ()):
                pl.when(b == bb)(lambda m=m: act(m))

    errands = {}
    for n in range(len(groups)):
        errands.setdefault(3 + n, []).append(("own", 0, n))
        for d in range(1, planes):
            errands.setdefault(min(3 + 3 * d + n, count), []).append(("far", d, n))

    def errand(e):
        kind, d, n = e
        if kind == "own":
            spread_own(n)
        else:
            spread_far(d, n)

    gains.wait()
    load_part(0).wait()
    for work in norm_first(0, 0):
        work()
    enter()
    for k in range(2):
        weight(0, k).wait()
    multiply_first(0, 0, head)
    for other in range(1, micro):
        load(other).start()
    for k in range(taps):
        weight(1, k).start()
    for k in range(2, taps):
        weight(0, k).wait()
    load_part(1).wait()

    @pl.loop(0, micro)
    def _(b):
        for t in range(parts):
            if t == 1:

                @pl.when(seq > 0)
                def _():
                    halo_up(b).wait_recv()

                @pl.when(seq < nseq - 1)
                def _():
                    halo_down(b).wait_recv()

            if t < parts - 1:
                multiply_first(b, t, tail, norm_first(b, t + 1))
                finish_first(b, t)
                multiply_first(b, t + 1, head)
            else:

                @pl.when(b < micro - 1)
                def _():
                    load(b + 1).wait()
                    multiply_first(b, t, tail, norm_first(b + 1, 0))
                    finish_first(b, t)
                    multiply_first(b + 1, 0, head)

                @pl.when(b == micro - 1)
                def _():
                    multiply_first(b, t, tail)
                    finish_first(b, t)

            at_step(b, t, {c: (c,) for c in range(4)}, direct)
            at_step(b, t, {p: (m,) for p, m in early.items()}, forward)
            at_step(b, t, errands, errand)
        for n in range(2):
            out_first(b, n).start()

    for m in between:
        forward(m)
    for k in range(taps):
        weight(1, k).wait()

    def step_second(b, t, more):
        norms = norm_second(b, t)
        for n in more:
            extra(b + 1, n, head, norms)
            norms = ()
            if n != more[-1]:
                extra(b + 1, n, tail)
                finish_extra(b + 1, n)
        for work in norms:
            work()
        multiply_second(b, t)
        if more:
            extra(b + 1, more[-1], tail)
        finish_second(b, t)
        if more:
            finish_extra(b + 1, more[-1])

    @pl.loop(0, micro)
    def _(b):
        for t in range(parts):
            at_step(b, t, late, forward)
            at_step(b, t, {1: errands.get(count, ())}, errand)
            at_step(b, t, {1: (0,)}, lambda _: swaps_done())
            arrived(b, t)
            if t == 0:
                pl.when((b > 0) & (b < micro - 1))(lambda: step_second(b, 0, (0,)))
                pl.when((b == 0) | (b == micro - 1))(lambda: step_second(b, 0, ()))
            elif t == 1:
                pl.when(b == 0)(lambda: step_second(b, 1, (0, 1)))
                pl.when((b > 0) & (b < micro - 1))(lambda: step_second(b, 1, (1,)))
                pl.when(b == micro - 1)(lambda: step_second(b, 1, ()))
            else:
                pl.when(b < micro - 1)(lambda: step_second(b, 2, (2,)))
                pl.when(b == micro - 1)(lambda: step_second(b, 2, ()))


    @pl.when(seq < nseq - 1)
    def _():
        for b in range(micro):
            halo_up(b).wait_send()

    @pl.when(seq > 0)
    def _():
        for b in range(micro):
            halo_down(b).wait_send()

    spread_sent()
    for c in range(count):
        send(me, c, 0, right).wait_send()
        send(me, c, 1, left).wait_send()
        send(left, c, 2, right).wait_send()
        send(right, c, 3, left).wait_send()

    @pl.loop(0, micro)
    def _(b):
        for n in range(2):
            out_first(b, n).wait()


def fused(inputs, weights, gains):
    micro, rows, chans = inputs.shape
    layers, taps, _, share = weights.shape
    span = rows + 2 * HALO
    count = len(chunk_ends(rows)) * micro
    ends = chunk_ends(rows)
    edges = [0] + [e + 32 for e in ends[:-1]] + [rows + 16]
    sizes = [q - p for p, q in zip(edges, edges[1:])]
    planes = lax.axis_size("seq") // 2
    dma = pltpu.SemaphoreType.DMA
    hbm = pl.BlockSpec(memory_space=pltpu.HBM)
    return pl.pallas_call(
        fused_kernel,
        out_shape=jax.ShapeDtypeStruct((layers, micro, rows, share), jnp.bfloat16),
        in_specs=[hbm, hbm, hbm],
        out_specs=pl.BlockSpec(memory_space=pltpu.VMEM),
        scratch_shapes=[
            pltpu.VMEM((micro, span, chans), jnp.bfloat16),
            *(pltpu.VMEM((micro, n, chans), jnp.bfloat16) for n in sizes),
            pltpu.VMEM((rows + HALO, chans), jnp.bfloat16),
            pltpu.VMEM((rows + 32, taps * share), jnp.float32),
            pltpu.VMEM((rows + 32, taps * EXTRA), jnp.float32),
            pltpu.VMEM((2, chans, taps * share), jnp.bfloat16),
            pltpu.VMEM((chans, taps * EXTRA), jnp.bfloat16),
            pltpu.VMEM(gains.shape, jnp.float32),
            pltpu.VMEM((4, micro, rows + HALO, share), jnp.bfloat16),
            dma,
            dma((2, taps)),
            dma((micro + 1,)),
            dma((2, micro)),
            dma((2, micro)),
            dma((4, count)),
            dma((4, count)),
            dma((micro, 2)),
            dma((taps,)),
            dma((taps,)),
            dma((2, planes, 2)),
            dma((planes, 2)),
            dma((planes, 2)),
            dma((planes, 2)),
        ],
        compiler_params=pltpu.CompilerParams(
            collective_id=0, has_side_effects=True, vmem_limit_bytes=50 * 1024 * 1024
        ),
    )(inputs, weights, gains)


def local(inputs, weights, gains):
    micro, rows, chans = inputs.shape
    layers, taps, _, share = weights.shape
    nseq = lax.axis_size("seq")
    square = lax.axis_size("section") == 4 and layers == 2 and nseq % 2 == 0 and nseq > 2
    wide = share % 128 == 0 and share > 2 * EXTRA and chans % (16 * nseq) == 0
    if square and wide and taps == 5 and micro > 1 and rows % 512 == 0:
        return fused(inputs, weights, gains)
    return plain(inputs, weights, gains)


def solution(mesh):
    in_specs = (P(None, "seq", None), P(None, None, None, "section"), P())
    out_specs = P(None, None, "seq", "section")
    return jax.shard_map(local, mesh=mesh, in_specs=in_specs, out_specs=out_specs, check_vma=False)
```

```python
import functools
import jax
import jax.numpy as jnp
from jax import lax
from jax.experimental import pallas as pl
from jax.experimental.pallas import tpu as pltpu
from jax.sharding import PartitionSpec as P

MESH = pl.DeviceIdType.MESH
HALO = 16
REACH = 2
EXTRA = 128


def with_halo(value, sides, width):
    for axis, dim in sides:
        count, length = (lax.axis_size(axis), value.shape[dim])
        up = [(i, (i + 1) % count) for i in range(count - 1)]
        down = [(j, i) for i, j in up]
        last = lax.slice_in_dim(value, length - width, length, axis=dim)
        initial = lax.slice_in_dim(value, 0, width, axis=dim)
        before = lax.ppermute(last, axis, up)
        after = lax.ppermute(initial, axis, down)
        value = jnp.concatenate([before, value, after], axis=dim)
    return value


def convolve(padded, kernel):
    count = padded.shape[1] - 4
    total = jnp.zeros((padded.shape[0], count, kernel.shape[2]), jnp.float32)
    for k in range(5):
        total = total + jnp.einsum(
            "brc,co->bro", padded[:, k : k + count], kernel[k], preferred_element_type=jnp.float32
        )
    return total


def normed(current, gain):
    values = current.astype(jnp.float32)
    scale = lax.rsqrt(jnp.mean(values * values, axis=-1, keepdims=True) + 1e-06)
    return jax.nn.gelu(values * scale * gain).astype(jnp.bfloat16)


def neighbours(hidden):
    return with_halo(hidden, (("seq", 1),), 2)


def plain(inputs, weights, gains):
    share = weights.shape[3]
    begin = lax.axis_index("section") * share
    hidden = normed(inputs, gains[0])
    conv = convolve(neighbours(hidden), weights[0])
    own = lax.dynamic_slice_in_dim(inputs, begin, share, 2)
    current = (own.astype(jnp.float32) + conv).astype(jnp.bfloat16)
    results = [current]
    kernel = weights[1]
    whole = lax.all_gather(current, "section", axis=2, tiled=True)
    conv = convolve(neighbours(normed(whole, gains[1])), kernel)
    current = (current.astype(jnp.float32) + conv).astype(jnp.bfloat16)
    results.append(current)
    return jnp.stack(results, axis=0)


def gelu_of_twice(h):
    return h + h * jnp.tanh(h * (1.5957691216057308 + 0.285419265090401 * (h * h)))


def chunk_ends(rows):
    tiles = rows // 16
    return [tiles * 11 // 32 * 16, tiles * 23 // 32 * 16, rows + 8]


def schedule(count):
    early = {5 + 2 * m: m for m in range(3)}
    between = [len(early)]
    late = {m - 2: (m,) for m in range(len(early) + 1, count)}
    return early, between, late


def fused_kernel(
    x, w, g, out, xe, hid_a, hid_b, hid_c, hid1, y, yx, wv, wx, gv, acts,
    gsem, wsem, xsem, hsend, hrecv, ssem, rsem, osem,
    tsend, trecv, zsend, zrecv, psend, precv,
):
    micro, rows, chans = x.shape
    taps, share = w.shape[1], w.shape[3]
    span = rows + 2 * HALO
    ends = chunk_ends(rows)
    begins = [0] + ends[:-1]
    parts = len(ends)
    count = parts * micro
    me, seq = lax.axis_index("section"), lax.axis_index("seq")
    nseq = lax.axis_size("seq")
    planes = nseq // 2
    plane, core = seq // 2, seq % 2
    partner = seq + 1 - 2 * core
    piece_rows = chans // nseq
    early, between, late = schedule(count)

    def ring(at):
        r = at // 2
        return 2 * r + (at % 2) * (1 - 2 * (r % 2)) + r % 2

    place = ring(me)
    right, left = ring((place + 1) % 4), ring((place + 3) % 4)
    over = ring((place + 2) % 4)

    gains = pltpu.make_async_copy(g, gv, gsem)

    def load(b):
        return pltpu.make_async_copy(x.at[b], xe.at[b, pl.ds(HALO, rows)], xsem.at[b])

    def weight(l, k):
        return pltpu.make_async_copy(w.at[l, k], wv.at[l, :, pl.ds(k * share, share)], wsem.at[l, k])

    def load_part(n):
        part = ((0, ends[0] + 64), (ends[0] + 64, rows))[n]
        size = part[1] - part[0]
        return pltpu.make_async_copy(
            x.at[0, pl.ds(part[0], size)], xe.at[0, pl.ds(HALO + part[0], size)], xsem.at[n * micro]
        )

    gains.start()
    load_part(0).start()
    for k in range(taps):
        weight(0, k).start()
    load_part(1).start()

    barrier = pltpu.get_barrier_semaphore()
    for to in (right, left):
        pl.semaphore_signal(barrier, inc=1, device_id=(to, seq), device_id_type=MESH)

    def greet(reach):
        @pl.when(seq >= reach)
        def _():
            pl.semaphore_signal(barrier, inc=1, device_id=(me, seq - reach), device_id_type=MESH)

        @pl.when(seq < nseq - reach)
        def _():
            pl.semaphore_signal(barrier, inc=1, device_id=(me, seq + reach), device_id_type=MESH)

    greet(1)
    greet(2)
    peers = 2
    for reach in (1, 2):
        peers = peers + jnp.where(seq >= reach, 1, 0) + jnp.where(seq < nseq - reach, 1, 0)
    def halo_up(b):
        return pltpu.make_async_remote_copy(
            src_ref=x.at[b, pl.ds(rows - HALO, HALO), :],
            dst_ref=xe.at[b, pl.ds(0, HALO), :],
            send_sem=hsend.at[0, b],
            recv_sem=hrecv.at[0, b],
            device_id=(me, seq + 1),
            device_id_type=MESH,
        )

    def halo_down(b):
        return pltpu.make_async_remote_copy(
            src_ref=x.at[b, pl.ds(0, HALO), :],
            dst_ref=xe.at[b, pl.ds(HALO + rows, HALO), :],
            send_sem=hsend.at[1, b],
            recv_sem=hrecv.at[1, b],
            device_id=(me, seq - 1),
            device_id_type=MESH,
        )

    def tap(k):
        return pltpu.make_async_remote_copy(
            src_ref=w.at[0, k, pl.ds(seq * piece_rows, piece_rows), pl.ds(0, EXTRA)],
            dst_ref=wx.at[pl.ds(seq * piece_rows, piece_rows), pl.ds(k * EXTRA, EXTRA)],
            send_sem=tsend.at[k],
            recv_sem=trecv.at[k],
            device_id=(right, seq),
            device_id_type=MESH,
        )

    groups = ((0, 3), (3, taps))

    def block(index, n):
        low, high = groups[n]
        return wx.at[
            pl.ds(pl.multiple_of(index * piece_rows, 8), piece_rows),
            pl.ds(low * EXTRA, (high - low) * EXTRA),
        ]

    def spread(at, n, way, to):
        source = 2 * at + core
        return pltpu.make_async_remote_copy(
            src_ref=block(source, n),
            dst_ref=block(source, n),
            send_sem=zsend.at[way, at, n],
            recv_sem=zrecv.at[at, n],
            device_id=(me, to),
            device_id_type=MESH,
        )

    def swap(at, n):
        source = 2 * at + core
        return pltpu.make_async_remote_copy(
            src_ref=block(source, n),
            dst_ref=block(source, n),
            send_sem=psend.at[at, n],
            recv_sem=precv.at[at, n],
            device_id=(me, partner),
            device_id_type=MESH,
        )

    def swapped(at, n):
        source = 2 * at + 1 - core
        return pltpu.make_async_remote_copy(
            src_ref=block(source, n),
            dst_ref=block(source, n),
            send_sem=psend.at[at, n],
            recv_sem=precv.at[at, n],
            device_id=(me, partner),
            device_id_type=MESH,
        )

    def spread_own(n):
        for k in range(*groups[n]):
            tap(k).wait_recv()

        @pl.when(plane < planes - 1)
        def _():
            spread(plane, n, 0, seq + 2).start()

        @pl.when(plane > 0)
        def _():
            spread(plane, n, 1, seq - 2).start()

        swap(plane, n).start()

    def spread_far(d, n):
        @pl.when(plane >= d)
        def _():
            spread(plane - d, n, 0, seq).wait_recv()

            @pl.when(plane < planes - 1)
            def _():
                spread(plane - d, n, 0, seq + 2).start()

            swap(plane - d, n).start()

        @pl.when(plane < planes - d)
        def _():
            spread(plane + d, n, 1, seq).wait_recv()

            @pl.when(plane > 0)
            def _():
                spread(plane + d, n, 1, seq - 2).start()

            swap(plane + d, n).start()

    def spread_sent():
        for n in range(len(groups)):
            for k in range(*groups[n]):
                tap(k).wait_send()
            for at in range(planes):
                swap(at, n).wait_send()

                @pl.when((plane >= at) & (plane < planes - 1))
                def _():
                    spread(at, n, 0, seq + 2).wait_send()

                @pl.when((plane <= at) & (plane > 0))
                def _():
                    spread(at, n, 1, seq - 2).wait_send()

    @pl.when(seq == 0)
    def _():
        xe[:, 0:HALO, :] = jnp.zeros((micro, HALO, chans), jnp.bfloat16)

    @pl.when(seq == nseq - 1)
    def _():
        xe[:, HALO + rows : span, :] = jnp.zeros((micro, HALO, chans), jnp.bfloat16)

    def enter():
        pl.semaphore_wait(barrier, peers)
        for k in range(taps):
            tap(k).start()

        @pl.when(seq < nseq - 1)
        def _():
            for b in range(micro):
                halo_up(b).start()

        @pl.when(seq > 0)
        def _():
            for b in range(micro):
                halo_down(b).start()

    def channels(way, whole):
        if whole:
            return ((0, share), (0, share), (2 * EXTRA, share), (0, 2 * EXTRA))[way]
        return ((EXTRA, share), (0, share), (EXTRA, share), (0, EXTRA))[way]

    def send(origin, c, way, to):
        b, t = c // parts, c % parts
        size = ends[t] - begins[t]
        low, high = channels(way, b == 0)
        ref = acts.at[origin, b, pl.ds(begins[t], size), pl.ds(low, high - low)]
        return pltpu.make_async_remote_copy(
            src_ref=ref,
            dst_ref=ref,
            send_sem=ssem.at[way, c],
            recv_sem=rsem.at[way, c],
            device_id=(to, seq),
            device_id_type=MESH,
        )

    def direct(c):
        send(me, c, 0, right).start()
        send(me, c, 1, left).start()

    def forward(c):
        send(left, c, 0, left).wait_recv()
        send(left, c, 2, right).start()
        send(right, c, 1, right).wait_recv()
        send(right, c, 3, left).start()
        for n in range(4, count):
            ahead = 2 if n == count - 1 else 3 if n == count - 2 else 4
            if c == n - ahead:
                direct(n)

    def arrived(b, t):
        pl.when(b == 0)(lambda: arrived_in(b, t, True))
        pl.when(b > 0)(lambda: arrived_in(b, t, False))

    def arrived_in(b, t, whole):
        size = ends[t] - begins[t]
        c = b * parts + t
        for way in (2, 3):
            low, high = channels(way, whole)
            ref = acts.at[over, b, pl.ds(begins[t], size), pl.ds(low, high - low)]
            pltpu.make_async_remote_copy(
                src_ref=ref,
                dst_ref=ref,
                send_sem=ssem.at[way, c],
                recv_sem=rsem.at[way, c],
                device_id=(right, seq),
                device_id_type=MESH,
            ).wait_recv()

    tile = 16

    def activate(v, l):
        scale = lax.rsqrt(jnp.mean(v * v, axis=-1, keepdims=True) + 1e-06)
        return gelu_of_twice(v * (0.5 * scale) * gv[l : l + 1, :]).astype(jnp.bfloat16)

    step = 512

    def product(dst, src, kernel, begin, end, wide, which=slice(None), beside=()):
        starts = list(range(0, wide, step))[which]
        for i, n in enumerate(starts):
            for tile_work in beside[i :: len(starts)]:
                tile_work()
            size = min(step, wide - n)
            dst[begin + 8 : end + 8, n : n + size] = jnp.dot(
                src(begin, end), kernel(n, size), preferred_element_type=jnp.float32
            )

    def close(dst):
        dst[0:8, :] = dst[rows + 16 : rows + 24, :]
        dst[rows + 24 : rows + 32, :] = dst[8:16, :]

    def gather_taps(src, u, width, stride):
        total = None
        block = src[u : u + tile + 16, :]
        for k in range(taps):
            term = block[8 - REACH + k : 8 - REACH + k + tile, k * stride : k * stride + width]
            total = term if total is None else total + term
        return total

    mine = pl.ds(pl.multiple_of(me * share, 128), share)
    theirs = pl.ds(pl.multiple_of(left * share, 128), EXTRA)

    def source(b, u, columns):
        if u == rows - 16:
            bottom = xe[b, HALO + rows : span, columns].astype(jnp.float32)
            top = xe[b, 0:HALO, columns].astype(jnp.float32)
            return jnp.concatenate([bottom[0:8, :], top[8:16, :]], axis=0)
        at = HALO if u == rows else 2 * HALO + u
        return xe[b, at : at + tile, columns].astype(jnp.float32)

    edges0 = [0] + [e + 2 * tile for e in ends[:-1]] + [rows + 16]

    hid = (hid_a, hid_b, hid_c)

    def norm_first(b, t):
        def work(u):
            at = u - edges0[t]
            hid[t][b, at : at + tile, :] = activate(source(b, u, slice(None)), 0)

        return [functools.partial(work, u) for u in range(edges0[t], edges0[t + 1], tile)]

    def outputs(edges, t):
        begin = tile if t == 0 else edges[t] - tile
        end = edges[t + 1] if t == parts - 1 else edges[t + 1] - tile
        return list(range(begin, end, tile)) + ([0] if t == parts - 1 else [])

    def conv_first(b, t, src, owner, columns, width, stride):
        for u in outputs(edges0, t):
            value = source(b, u, columns) + gather_taps(src, u, width, stride)
            at = u - tile
            if u == rows - 16:
                at = rows
                row = lax.broadcasted_iota(jnp.int32, (8, width), 0)
                value = jnp.where(row < 4, value[0:8, :], value[8:16, :])
                inside = ((row < 4) & (seq < nseq - 1)) | ((row >= 4) & (seq > 0))
                value = jnp.where(inside, value, 0.0)
                value = jnp.concatenate([value, jnp.zeros_like(value)], axis=0)
            elif u == rows:
                at = rows - 32
            elif u == 0:
                at = rows - 16
            acts[owner, b, at : at + tile, 0:width] = value.astype(jnp.bfloat16)

    def multiply_first(b, t, which, beside=()):
        product(
            y, lambda p, q: hid[t][b], lambda n, s: wv[0, :, n : n + s],
            edges0[t], edges0[t + 1], taps * share, which, beside,
        )

    def finish_first(b, t):
        if t == parts - 1:
            close(y)
        conv_first(b, t, y, me, mine, share, share)

    head, tail = slice(0, 1), slice(1, None)

    def extra(b, t, which, beside=()):
        product(
            yx, lambda p, q: hid[t][b], lambda n, s: wx[:, n : n + s],
            edges0[t], edges0[t + 1], taps * EXTRA, which, beside,
        )

    def finish_extra(b, t):
        if t == parts - 1:
            close(yx)
        conv_first(b, t, yx, left, theirs, EXTRA, EXTRA)

    edges1 = [0] + ends[:-1] + [rows + 16]

    def held(u):
        return u if u < rows - 32 else rows if u == rows - 32 else u - 16

    def norm_second(b, t):
        def work(u):
            at = held(u)
            pieces = [acts[s, b, at : at + tile, :].astype(jnp.float32) for s in range(4)]
            value = jnp.concatenate(pieces, axis=-1)
            if at == rows:
                value = jnp.concatenate([value[0:8, :], value[0:8, :]], axis=0)
            hid1[u : u + tile, :] = activate(value, 1)

        return [functools.partial(work, u) for u in range(edges1[t], edges1[t + 1], tile)]

    def multiply_second(b, t, beside=()):
        product(
            y, lambda p, q: hid1[p:q, :], lambda n, s: wv[1, :, n : n + s],
            edges1[t], edges1[t + 1], taps * share, beside=beside,
        )

    def finish_second(b, t):
        if t == parts - 1:
            close(y)
        for u in outputs(edges1, t):
            if u == rows - 32:
                continue
            at = held(u)
            value = acts[me, b, at : at + tile, :].astype(jnp.float32)
            value = value + gather_taps(y, u, share, share)
            row = u + 32 if u < rows - 32 else u - (rows - 16)
            out[1, b, row : row + tile, :] = value.astype(jnp.bfloat16)

    def out_first(b, n):
        begin, size, row = ((0, rows - 32, 32), (rows - 32, 32, 0))[n]
        return pltpu.make_async_copy(
            acts.at[me, b, pl.ds(begin, size), :], out.at[0, b, pl.ds(row, size)], osem.at[b, n]
        )

    def swaps_done():
        for n in range(len(groups)):
            for at in range(planes):
                swapped(at, n).wait_recv()

    def at_step(b, t, table, act):
        for bb in range(micro):
            for m in table.get(bb * parts + t, ()):
                pl.when(b == bb)(lambda m=m: act(m))

    errands = {}
    for n in range(len(groups)):
        errands.setdefault(3 + n, []).append(("own", 0, n))
        for d in range(1, planes):
            errands.setdefault(min(3 + 3 * d + n, count), []).append(("far", d, n))

    def errand(e):
        kind, d, n = e
        if kind == "own":
            spread_own(n)
        else:
            spread_far(d, n)

    gains.wait()
    load_part(0).wait()
    for work in norm_first(0, 0):
        work()
    enter()
    for k in range(2):
        weight(0, k).wait()
    multiply_first(0, 0, head)
    for other in range(1, micro):
        load(other).start()
    for k in range(taps):
        weight(1, k).start()
    for k in range(2, taps):
        weight(0, k).wait()
    load_part(1).wait()

    @pl.loop(0, micro)
    def _(b):
        for t in range(parts):
            if t == 1:

                @pl.when(seq > 0)
                def _():
                    halo_up(b).wait_recv()

                @pl.when(seq < nseq - 1)
                def _():
                    halo_down(b).wait_recv()

            if t < parts - 1:
                multiply_first(b, t, tail, norm_first(b, t + 1))
                finish_first(b, t)
                multiply_first(b, t + 1, head)
            else:

                @pl.when(b < micro - 1)
                def _():
                    load(b + 1).wait()
                    multiply_first(b, t, tail, norm_first(b + 1, 0))
                    finish_first(b, t)
                    multiply_first(b + 1, 0, head)

                @pl.when(b == micro - 1)
                def _():
                    multiply_first(b, t, tail)
                    finish_first(b, t)

            at_step(b, t, {c: (c,) for c in range(4)}, direct)
            at_step(b, t, {p: (m,) for p, m in early.items()}, forward)
            at_step(b, t, errands, errand)
        for n in range(2):
            out_first(b, n).start()

    for m in between:
        forward(m)
    for k in range(taps):
        weight(1, k).wait()

    def step_second(b, t, more):
        norms = norm_second(b, t)
        for n in more:
            extra(b + 1, n, head, norms)
            norms = ()
            if n != more[-1]:
                extra(b + 1, n, tail)
                finish_extra(b + 1, n)
        for work in norms:
            work()
        multiply_second(b, t)
        if more:
            extra(b + 1, more[-1], tail)
        finish_second(b, t)
        if more:
            finish_extra(b + 1, more[-1])

    @pl.loop(0, micro)
    def _(b):
        for t in range(parts):
            at_step(b, t, late, forward)
            at_step(b, t, {1: errands.get(count, ())}, errand)
            at_step(b, t, {1: (0,)}, lambda _: swaps_done())
            arrived(b, t)
            if t == 0:
                pl.when((b > 0) & (b < micro - 1))(lambda: step_second(b, 0, (0,)))
                pl.when((b == 0) | (b == micro - 1))(lambda: step_second(b, 0, ()))
            elif t == 1:
                pl.when(b == 0)(lambda: step_second(b, 1, (0, 1)))
                pl.when((b > 0) & (b < micro - 1))(lambda: step_second(b, 1, (1,)))
                pl.when(b == micro - 1)(lambda: step_second(b, 1, ()))
            else:
                pl.when(b < micro - 1)(lambda: step_second(b, 2, (2,)))
                pl.when(b == micro - 1)(lambda: step_second(b, 2, ()))


    @pl.when(seq < nseq - 1)
    def _():
        for b in range(micro):
            halo_up(b).wait_send()

    @pl.when(seq > 0)
    def _():
        for b in range(micro):
            halo_down(b).wait_send()

    spread_sent()
    for c in range(count):
        send(me, c, 0, right).wait_send()
        send(me, c, 1, left).wait_send()
        send(left, c, 2, right).wait_send()
        send(right, c, 3, left).wait_send()

    @pl.loop(0, micro)
    def _(b):
        for n in range(2):
            out_first(b, n).wait()


def fused(inputs, weights, gains):
    micro, rows, chans = inputs.shape
    layers, taps, _, share = weights.shape
    span = rows + 2 * HALO
    count = len(chunk_ends(rows)) * micro
    ends = chunk_ends(rows)
    edges = [0] + [e + 32 for e in ends[:-1]] + [rows + 16]
    sizes = [q - p for p, q in zip(edges, edges[1:])]
    planes = lax.axis_size("seq") // 2
    dma = pltpu.SemaphoreType.DMA
    hbm = pl.BlockSpec(memory_space=pltpu.HBM)
    return pl.pallas_call(
        fused_kernel,
        out_shape=jax.ShapeDtypeStruct((layers, micro, rows, share), jnp.bfloat16),
        in_specs=[hbm, hbm, hbm],
        out_specs=pl.BlockSpec(memory_space=pltpu.VMEM),
        scratch_shapes=[
            pltpu.VMEM((micro, span, chans), jnp.bfloat16),
            *(pltpu.VMEM((micro, n, chans), jnp.bfloat16) for n in sizes),
            pltpu.VMEM((rows + HALO, chans), jnp.bfloat16),
            pltpu.VMEM((rows + 32, taps * share), jnp.float32),
            pltpu.VMEM((rows + 32, taps * EXTRA), jnp.float32),
            pltpu.VMEM((2, chans, taps * share), jnp.bfloat16),
            pltpu.VMEM((chans, taps * EXTRA), jnp.bfloat16),
            pltpu.VMEM(gains.shape, jnp.float32),
            pltpu.VMEM((4, micro, rows + HALO, share), jnp.bfloat16),
            dma,
            dma((2, taps)),
            dma((micro + 1,)),
            dma((2, micro)),
            dma((2, micro)),
            dma((4, count)),
            dma((4, count)),
            dma((micro, 2)),
            dma((taps,)),
            dma((taps,)),
            dma((2, planes, 2)),
            dma((planes, 2)),
            dma((planes, 2)),
            dma((planes, 2)),
        ],
        compiler_params=pltpu.CompilerParams(
            collective_id=0, has_side_effects=True, vmem_limit_bytes=50 * 1024 * 1024
        ),
    )(inputs, weights, gains)


def local(inputs, weights, gains):
    micro, rows, chans = inputs.shape
    layers, taps, _, share = weights.shape
    nseq = lax.axis_size("seq")
    square = lax.axis_size("section") == 4 and layers == 2 and nseq % 2 == 0 and nseq > 2
    wide = share % 128 == 0 and share > 2 * EXTRA and chans % (16 * nseq) == 0
    if square and wide and taps == 5 and micro > 1 and rows % 512 == 0:
        return fused(inputs, weights, gains)
    return plain(inputs, weights, gains)


def solution(mesh):
    in_specs = (P(None, "seq", None), P(None, None, None, "section"), P())
    out_specs = P(None, None, "seq", "section")
    return jax.shard_map(local, mesh=mesh, in_specs=in_specs, out_specs=out_specs, check_vma=False)
```
